128 devices in a mesh: row: 8 (over x, core), col: 16 (over z, y).
Axes of the slice: x: 4, y: 4, z: 4, core: 2. Of those that a mesh axis runs over, the one named last changes fastest.
Arguments:
- ham: bfloat16 [6144, 6144], P('row', 'col'), may hold values from -0.078125 to 0.078125
- deriv: bfloat16 [6144, 6144], P('row', 'col'), may hold values from -6 to 6
- band: int32 [48], replicated, may hold values from 1 to 24, as said below
- frag_of: int32 [48], replicated, may hold values from 0 to 31
Outputs:
- sign_iterate: bfloat16 [6144, 6144], P('row', 'col')
- energy_density: bfloat16 [6144, 6144], P('row', 'col')
- pulay_terms: float32 [32, 128], P('col')
The draws below stay inside these ranges and needn't reach their ends.
Inputs may be any that keep to these rules, and one draw needn't show every extreme that they name: Some block row has band half-width exactly 24.
All inputs are finite; a program needn't handle non-finite values.
Results may differ from the reference program's by a relative error of at most 0.006.
Values may be sent and summed in bfloat16 or wider, within the bound.
A program may use at most 64 MiB of HBM per device.

```python
import jax
import jax.numpy as jnp
from jax import lax

BLK = 128
WMIN = 1
NB = 48
WMAX = 24
ORDER = 6144
FRAGS = 32


def draw_band(key, part):
    first_key = jax.random.fold_in(key, 11)
    second_key = jax.random.fold_in(key, 23)
    widths = jax.random.randint(first_key, (NB,), WMIN, WMAX + 1, dtype=jnp.int32)
    chosen = jax.random.randint(second_key, (), 0, NB, dtype=jnp.int32)
    places = jnp.arange(NB, dtype=jnp.int32)
    return jnp.where(places == chosen, jnp.int32(WMAX), widths).astype(jnp.int32)


def place_ends(values, own_key, low, high):
    place = [jax.random.randint(jax.random.fold_in(own_key, axis), (), 0, length) for axis, length in enumerate(values.shape)]
    longest = values.shape.index(max(values.shape))
    neighbour = place[:longest] + [(place[longest] + 1) % values.shape[longest]] + place[longest + 1:]
    return values.at[tuple(place)].set(low).at[tuple(neighbour)].set(high)


def block_levels(rng, extent, cuts, least, top_value):
    gain = 1.0
    for position, shards_of in cuts:
        draws = jax.random.uniform(jax.random.fold_in(jax.random.fold_in(rng, 6), position), (shards_of,), jnp.float32, least / len(cuts), top_value / len(cuts))
        gain = gain * jnp.repeat(jnp.exp(draws), extent[position] // shards_of).reshape((-1,) + (1,) * (len(extent) - 1 - position))
    return gain


def gaussian(key, extent, width, limit, shards=(), kind=jnp.bfloat16):
    result = jax.random.normal(key, extent, jnp.float32) * width
    if len(shards) > 0:
        result = block_levels(key, extent, shards, -0.22, 0.18) * result
    return jnp.clip(result, min=-limit, max=limit).astype(kind)


def setup_inputs(seed: int = 0) -> dict:
    streams_of = jax.random.split(jax.random.key(seed), 5)
    ham = gaussian(streams_of[0], (ORDER, ORDER), (BLK * (2 * WMAX + 1)) ** -0.5, 0.078125, ((0, 8), (1, 16)))
    deriv = gaussian(streams_of[1], (ORDER, ORDER), 1.0, 6.0, ((0, 8), (1, 16)))
    band = draw_band(jax.random.fold_in(streams_of[4], 71), 0)
    frag_of = place_ends(jax.random.randint(streams_of[3], (NB,), 0, FRAGS), jax.random.fold_in(streams_of[3], 1), 0, FRAGS - 1).astype(jnp.int32)
    return dict(ham=ham, deriv=deriv, band=band, frag_of=frag_of)


def pattern_of(band):
    blocks = jnp.arange(NB, dtype=jnp.int32)
    widest = jnp.maximum(band[:, None], band[None, :])
    inside = jnp.abs(blocks[:, None] - blocks[None, :]) <= widest
    block_mask = inside.astype(jnp.float32)
    return jnp.repeat(jnp.repeat(block_mask, BLK, axis=0), BLK, axis=1)


def reference(ham, deriv, band, frag_of):
    pattern = pattern_of(band)
    start = (ham.astype(jnp.float32) * pattern).astype(jnp.bfloat16)
    square = (jnp.dot(start, start, preferred_element_type=jnp.float32) * pattern).astype(jnp.bfloat16)
    cubic = jnp.dot(start, square, preferred_element_type=jnp.float32)
    sign_iterate = (pattern * (1.5 * start.astype(jnp.float32) - 0.5 * cubic)).astype(jnp.bfloat16)
    identity = jnp.eye(ORDER, dtype=jnp.float32)
    density = (0.5 * (identity - sign_iterate.astype(jnp.float32))).astype(jnp.bfloat16)
    weighted = (jnp.dot(start, density, preferred_element_type=jnp.float32) * pattern).astype(jnp.bfloat16)
    energy_density = (jnp.dot(density, weighted, preferred_element_type=jnp.float32) * pattern).astype(jnp.bfloat16)
    column_terms = jnp.sum(energy_density.astype(jnp.float32) * deriv.astype(jnp.float32), axis=0).reshape(NB, BLK)
    fragments = jnp.arange(FRAGS, dtype=jnp.int32)
    onehot = (frag_of[None, :] == fragments[:, None]).astype(jnp.float32)
    pulay_terms = jnp.dot(onehot, column_terms, precision=lax.Precision.HIGHEST)
    return sign_iterate, energy_density, pulay_terms
```

```python
import functools

import jax
import jax.numpy as jnp
from jax import lax
from jax.experimental import pallas as pl
from jax.experimental.pallas import tpu as pltpu
from jax.sharding import PartitionSpec as P

MESH = pl.DeviceIdType.MESH
BLK = 128
ROWS = 768
COLS = 384
NR = 8
NC = 16
F32 = jnp.float32
BF16 = jnp.bfloat16
OFFS = (0, 256, 512, 640)
HALF = (128, 128, 64, 64)
ORDER = (
    "RaS0", "RaS1", "RaS2", "LaS0", "LaS1", "prep", "LbS0", "RbS0", "RaS3", "LbS1", "LcS0", "LaS2",
    "LcS1", "LaS3", "RbS1", "RbS2", "RcS0", "RdS0", "RbS3", "LdS0", "LbS2", "RcS1", "RcS2", "RdS1",
    "RcS3", "RdS2", "RdS3", "LdS1", "LbS3", "LeS0", "P1_0", "LcS2", "RaQ0", "LeS1", "P1_1", "LcS3",
    "RaQ1", "RbQ0", "LdS2", "RbQ1", "LdS3", "RcQ0", "LeS2", "P1_2", "RdQ0", "RaQ2", "RcQ1", "P2_00",
    "LeS3", "P1_3", "RaQ3", "RdQ1", "P2_01", "P2_10", "RbQ2", "P2_11", "P2_20", "P2_21", "RbQ3", "RcQ2",
    "RdQ2", "P2_02", "RcQ3", "P2_12", "P2_22", "RdQ3", "P2_03", "N0", "RaD0", "LaD0", "P2_13", "N1",
    "RaD1", "LaD1", "P2_23", "N2", "RaD2", "N3", "LbD0", "RbD0", "LbD1", "RaD3", "LcD0", "LaD2",
    "LcD1", "LaD3", "RbD1", "RbD2", "RcD0", "RdD0", "P3_00", "LdD0", "RbD3", "P3_10", "LbD2", "P3_20",
    "RcD1", "RcD2", "RcD3", "RdD1", "P3_01", "RdD2", "P3_02", "P3_11", "RdD3", "P3_03", "W0", "RaW0",
    "P3_12", "P3_13", "W1", "RaW1", "P3_21", "P3_22", "P3_23", "W2", "LdD1", "RaW2", "LbD3", "RbW0",
    "RaW3", "LeD0", "LcD2", "RbW1", "RbW2", "LeD1", "LcD3", "RcW0", "RdW0", "P4_00", "RbW3", "P4_10",
    "LdD2", "RcW1", "RcW2", "RdW1", "P4_01", "RdW2", "RcW3", "P4_02", "P4_11", "LdD3", "P4_12", "RdW3",
    "P4_03", "E0", "P4_13", "LeD2", "P4_2", "E2", "E1", "LeD3", "P4_3", "E3",
)


def kernel(band, frag, ham, deriv, n_out, e_out, pulay, ls, ld, rs, rq, rd, rw, mask, acc, terms, mine, by_row, by_col,
           weights, l_send, l_recv, r_send, r_recv, t_send, t_recv):
    r = lax.axis_index("row")
    c = lax.axis_index("col")
    z = lax.div(c, 4)
    y = lax.rem(c, 4)
    up = {"y": lax.rem(y + 1, 4), "z": lax.rem(z + 1, 4)}
    down = {"y": lax.rem(y + 3, 4), "z": lax.rem(z + 3, 4)}
    to = {
        ("y", 0): (r, z * 4 + up["y"]),
        ("y", 1): (r, z * 4 + down["y"]),
        ("z", 0): (r, up["z"] * 4 + y),
        ("z", 1): (r, down["z"] * 4 + y),
        ("x", 0): (lax.rem(r + 2, NR), c),
        ("x", 1): (lax.rem(r + 6, NR), c),
        "core": (r + 1 - 2 * lax.rem(r, 2), c),
    }
    r_up, r_down, r_far = lax.rem(r + 2, NR), lax.rem(r + 6, NR), lax.rem(r + 4, NR)

    barrier = pltpu.get_barrier_semaphore()
    for k in range(1, NR):
        pl.semaphore_signal(barrier, inc=1, device_id=(lax.rem(r + k, NR), c), device_id_type=MESH)
    for k in range(1, NC):
        pl.semaphore_signal(barrier, inc=1, device_id=(r, lax.rem(c + k, NC)), device_id_type=MESH)

    sent = []
    flying = {}

    def send(key, ref, target, send_sem, recv_sem):
        copy = pltpu.make_async_remote_copy(
            src_ref=ref, dst_ref=ref, send_sem=send_sem, recv_sem=recv_sem, device_id=target, device_id_type=MESH
        )
        copy.start()
        sent.append(copy)
        flying[key] = copy

    def landed(key):
        flying[key].wait_recv()

    left = {"S": ls, "D": ld}
    right = {"S": rs, "Q": rq, "D": rd, "W": rw}

    def left_send(x, p, stage, first, side, ref):
        axis = {"A": "yz", "B": "zy"}[first][0 if stage in "ab" else 1]
        i = ((("SD".index(x) * 4 + p) * 4 + "abcd".index(stage)) * 2 + "AB".index(first)) * 2 + side
        send((x, p, stage, first, side), ref, to[axis, side], l_send.at[i], l_recv.at[i])

    def left_wait(x, p, stage):
        for first in "AB":
            for side in (0, 1):
                landed((x, p, stage, first, side))

    def left_step(stage, x, p):
        buf, h, a = left[x], HALF[p], OFFS[p]
        if stage != "a":
            left_wait(x, p, "abcd"["bcde".index(stage)])
        for first in "AB":
            lo = a if first == "A" else a + h
            every = pl.ds(lo, h)
            parts = (pl.ds(lo, h // 2), pl.ds(lo + h // 2, h // 2))
            for side in (0, 1):
                back = (down, up)[side]
                if stage == "a":
                    ref = buf.at[z, y, every]
                elif stage == "b":
                    ref = buf.at[z, back["y"], parts[side]] if first == "A" else buf.at[back["z"], y, parts[side]]
                elif stage == "c":
                    ref = buf.at[z, :, every] if first == "A" else buf.at[:, y, every]
                elif stage == "d":
                    ref = buf.at[back["z"], :, parts[side]] if first == "A" else buf.at[:, back["y"], parts[side]]
                else:
                    return
                left_send(x, p, stage, first, side, ref)

    def right_send(x, p, kind, ref, target):
        i = ("SQDW".index(x) * 4 + p) * 8 + kind
        send((x, p, kind), ref, target, r_send.at[i], r_recv.at[i])

    def right_step(stage, x, p):
        buf, a, n = right[x], OFFS[p], 2 * HALF[p]
        rows = pl.ds(a, n)
        if stage == "a":
            right_send(x, p, 0, buf.at[r, rows], to["x", 0])
            right_send(x, p, 1, buf.at[r, rows], to["x", 1])
            right_send(x, p, 4, buf.at[r, rows], to["core"])
        elif stage == "b":
            landed((x, p, 0))
            landed((x, p, 1))
            right_send(x, p, 2, buf.at[r_down, pl.ds(a, n // 2)], to["x", 0])
            right_send(x, p, 3, buf.at[r_up, pl.ds(a + n // 2, n // 2)], to["x", 1])
            right_send(x, p, 5, buf.at[r_down, rows], to["core"])
            right_send(x, p, 6, buf.at[r_up, rows], to["core"])
        elif stage == "c":
            landed((x, p, 2))
            landed((x, p, 3))
            right_send(x, p, 7, buf.at[r_far, rows], to["core"])
        else:
            for kind in (4, 5, 6, 7):
                landed((x, p, kind))

    def whole(buf, panel, a, n):
        rows = pl.ds(a, n)
        acc[rows, :] = jnp.zeros((n, COLS), F32)

        def step(i, _):
            lhs = jnp.concatenate([buf[i, j, rows, :] for j in range(4)], axis=1)
            rhs = panel[pl.ds(2 * i, 2)].reshape(4 * COLS, COLS)
            acc[rows, :] += jnp.dot(lhs, rhs, preferred_element_type=F32)
            return 0

        lax.fori_loop(0, 4, step, 0)

    def part(buf, panel, a, n, q):
        rows = pl.ds(a, n)
        lo, size = OFFS[q], 2 * HALF[q]
        group = 1024 // size

        def piece(i, j):
            zz = i * (group // 2) + j // 2
            cols = []
            for half in (0, 1):
                s, e = max(lo, half * COLS), min(lo + size, (half + 1) * COLS)
                if s < e:
                    cols.append(buf[zz, 2 * (j % 2) + half, rows, s - half * COLS : e - half * COLS])
            return cols

        def step(i, _):
            lhs = jnp.concatenate([v for j in range(group) for v in piece(i, j)], axis=1)
            rhs = panel[pl.ds(group * i, group), pl.ds(lo, size), :].reshape(1024, COLS)
            acc[rows, :] += jnp.dot(lhs, rhs, preferred_element_type=F32)
            return 0

        if q == 0:
            acc[rows, :] = jnp.zeros((n, COLS), F32)
        if NR == group:
            step(0, 0)
        else:
            lax.fori_loop(0, NR // group, step, 0)

    def begin():
        for i in range(6):
            for j in range(3):
                row, col = r * 6 + i, c * 3 + j
                inside = jnp.abs(row - col) <= jnp.maximum(band[row], band[col])
                mask[pl.ds(i * BLK, BLK), pl.ds(j * BLK, BLK)] = jnp.full((BLK, BLK), jnp.where(inside, 1.0, 0.0), F32)
        start = (ham[...].astype(F32) * mask[...]).astype(BF16)
        rs[r] = start
        ls[z, y] = start
        mine[...] = jnp.zeros((8, BLK), F32)
        terms[...] = jnp.zeros((8, COLS), F32)
        pl.semaphore_wait(barrier, NR + NC - 2)

    def prepare():
        line = lax.broadcasted_iota(jnp.int32, (8, BLK), 0)
        for f in (0, 1):
            for k in range(NC):
                tile = jnp.zeros((8, BLK), F32)
                for m in range(3):
                    tile = jnp.where(line == m, jnp.where(frag[3 * k + m] == 2 * c + f, 1.0, 0.0), tile)
                weights[f, k] = tile

    def square_rows(p):
        a, n = OFFS[p], 2 * HALF[p]
        whole(ls, rs, a, n)
        rq[r, pl.ds(a, n), :] = (acc[pl.ds(a, n), :] * mask[pl.ds(a, n), :]).astype(BF16)

    def density_rows(p):
        a, n = OFFS[p], 2 * HALF[p]
        rows = pl.ds(a, n)
        sign = 1.5 * rs[r, rows, :].astype(F32) - 0.5 * acc[rows, :]
        sign = (mask[rows, :] * sign).astype(BF16)
        n_out[rows, :] = sign
        line = r * ROWS + a + lax.broadcasted_iota(jnp.int32, (n, COLS), 0)
        column = c * COLS + lax.broadcasted_iota(jnp.int32, (n, COLS), 1)
        identity = jnp.where(line == column, 1.0, 0.0)
        density = (0.5 * (identity - sign.astype(F32))).astype(BF16)
        rd[r, rows, :] = density
        ld[z, y, rows, :] = density

    def weighted_rows(u):
        rows = pl.ds(256 * u, 256)
        rw[r, rows, :] = (acc[rows, :] * mask[rows, :]).astype(BF16)

    def energy_rows(p):
        a, n = OFFS[p], 2 * HALF[p]
        rows = pl.ds(a, n)
        energy = (acc[rows, :] * mask[rows, :]).astype(BF16)
        e_out[rows, :] = energy
        product = energy.astype(F32) * deriv[rows, :].astype(F32)
        terms[...] += jnp.sum(product.reshape(n // 8, 8, COLS), axis=0)

    def finish():
        total = jnp.sum(terms[...], axis=0, keepdims=True)
        for m in range(3):
            mine[pl.ds(m, 1), :] = total[:, m * BLK : (m + 1) * BLK]
        by_row[r] = mine[...]
        first = []
        for k in range(1, NR):
            copy = pltpu.make_async_remote_copy(
                src_ref=mine, dst_ref=by_row.at[r], send_sem=t_send.at[k - 1], recv_sem=t_recv.at[k - 1],
                device_id=(lax.rem(r + k, NR), c), device_id_type=MESH,
            )
            copy.start()
            first.append(copy)
        for copy in first:
            copy.wait_recv()
        by_col[c] = jnp.sum(by_row[...], axis=0)
        second = []
        for k in range(1, NC):
            copy = pltpu.make_async_remote_copy(
                src_ref=by_col.at[c], dst_ref=by_col.at[c], send_sem=t_send.at[6 + k], recv_sem=t_recv.at[6 + k],
                device_id=(r, lax.rem(c + k, NC)), device_id_type=MESH,
            )
            copy.start()
            second.append(copy)
        for copy in second:
            copy.wait_recv()
        for f in (0, 1):
            picked = jnp.sum(weights[f] * by_col[...], axis=0)
            pulay[pl.ds(f, 1), :] = jnp.sum(picked, axis=0, keepdims=True)
        for copy in sent + first + second:
            copy.wait_send()

    begin()
    for name in ORDER:
        digits = [int(d) for d in name if d.isdigit()]
        if name[0] == "L":
            left_step(name[1], name[2], digits[0])
        elif name[0] == "R":
            right_step(name[1], name[2], digits[0])
        elif name[:2] == "P1":
            square_rows(digits[1])
        elif name[:2] in ("P2", "P3", "P4"):
            buf, panel = {"P2": (ls, rq), "P3": (ls, rd), "P4": (ld, rw)}[name[:2]]
            if len(digits) == 2:
                whole(buf, panel, OFFS[digits[1]], 2 * HALF[digits[1]])
            else:
                part(buf, panel, 256 * digits[1], 256, digits[2])
        elif name[0] == "N":
            density_rows(digits[0])
        elif name[0] == "W":
            weighted_rows(digits[0])
        elif name[0] == "E":
            energy_rows(digits[0])
        else:
            prepare()
    finish()


def step(ham, deriv, band, frag_of):
    vmem = pl.BlockSpec(memory_space=pltpu.VMEM)
    smem = pl.BlockSpec(memory_space=pltpu.SMEM)
    dma = pltpu.SemaphoreType.DMA
    panel = pltpu.VMEM((NR, ROWS, COLS), BF16)
    slab = pltpu.VMEM((4, 4, ROWS, COLS), BF16)
    return pl.pallas_call(
        kernel,
        out_shape=(
            jax.ShapeDtypeStruct((ROWS, COLS), BF16),
            jax.ShapeDtypeStruct((ROWS, COLS), BF16),
            jax.ShapeDtypeStruct((2, BLK), F32),
        ),
        in_specs=[smem, smem, vmem, vmem],
        out_specs=(vmem, vmem, vmem),
        scratch_shapes=[
            slab, slab, panel, panel, panel, panel,
            pltpu.VMEM((ROWS, COLS), F32),
            pltpu.VMEM((ROWS, COLS), F32),
            pltpu.VMEM((8, COLS), F32),
            pltpu.VMEM((8, BLK), F32),
            pltpu.VMEM((NR, 8, BLK), F32),
            pltpu.VMEM((NC, 8, BLK), F32),
            pltpu.VMEM((2, NC, 8, BLK), F32),
            dma((128,)), dma((128,)), dma((128,)), dma((128,)), dma((22,)), dma((22,)),
        ],
        compiler_params=pltpu.CompilerParams(collective_id=0, has_side_effects=True, vmem_limit_bytes=60 << 20),
        name="sign_step",
    )(band, frag_of, ham, deriv)


def solution(mesh):
    return jax.shard_map(
        step,
        mesh=mesh,
        in_specs=(P("row", "col"), P("row", "col"), P(), P()),
        out_specs=(P("row", "col"), P("row", "col"), P("col", None)),
        check_vma=False,
    )
```

```python
import functools

import jax
import jax.numpy as jnp
from jax import lax
from jax.experimental import pallas as pl
from jax.experimental.pallas import tpu as pltpu
from jax.sharding import PartitionSpec as P

MESH = pl.DeviceIdType.MESH
BLK = 128
ROWS = 768
COLS = 384
NR = 8
NC = 16
F32 = jnp.float32
BF16 = jnp.bfloat16
OFFS = (0, 256, 512, 640)
HALF = (128, 128, 64, 64)
NP = len(HALF)
LAST = NP - 1
PART = ((0, 256), (256, 256), (512, 128), (640, 128))
ORDER = (
    "LaS0", "LaS1", "prep", "RaS0", "RaS1", "RaS2", "LbS0", "RbS0", "RbS1", "LcS0", "LbS1", "RbS2",
    "RcS0", "RdS0", "RcS1", "RaS3", "LdS0", "RcS2", "RdS1", "LcS1", "LaS2", "LaS3", "RdS2", "RbS3",
    "RcS3", "RdS3", "LeS0", "P1_0", "LdS1", "RaQ0", "LbS2", "LbS3", "RbQ0", "LeS1", "P1_1", "LcS2",
    "RcQ0", "RaQ1", "LcS3", "RdQ0", "P2_00", "P2_10", "LdS2", "LdS3", "P1e_3", "RbQ1", "LeS2", "P1_2",
    "RaQ2", "LeS3", "P1_3", "RaQ3", "RcQ1", "P2_20", "RdQ1", "P2_21", "P2_11", "RbQ2", "P2_01", "RbQ3",
    "RcQ2", "RdQ2", "P2_12", "RcQ3", "P2_22", "P2_02", "RdQ3", "P2_13", "N1", "RaD1", "LaD1", "P2_03",
    "N0", "LaD0", "RaD0", "P2_23", "N2", "RaD2", "N3", "LaD3", "RaD3", "RbD1", "RbD0", "LbD0",
    "RbD2", "LcD0", "LbD1", "RbD3", "RcD1", "RdD1", "RcD0", "RcD2", "LdD0", "RdD0", "P3_00", "RcD3",
    "P3_01", "RdD2", "P3_02", "RdD3", "P3_03", "W0", "RaW0", "P3_10", "P3_11", "P3_12", "P3_13", "W1",
    "RaW1", "LcD1", "LaD2", "P3_20", "P3_21", "P3_22", "P3_23", "W2", "RbW0", "LeD0", "LdD1", "RbW1",
    "RaW2", "RaW3", "LbD2", "LbD3", "RcW0", "RdW0", "P4_00", "RcW1", "LeD1", "P4_10", "LcD2", "RdW1",
    "P4_01", "P4_11", "LcD3", "RbW2", "RbW3", "RcW2", "LdD2", "RcW3", "LdD3", "RdW2", "P4_02", "P4_12",
    "RdW3", "P4_03", "E0", "P4_13", "P4e_3", "LeD2", "P4_2", "E2", "LeD3", "P4_3", "E3", "E1",
)
FIRST = next(int(name[1]) for name in ORDER if name[0] == "E")


def kernel(band, frag, ham, deriv, n_out, e_out, pulay, ls, ld, rs, rq, rd, rw, mask, acc, terms, mine, by_row, by_col,
           weights, fetched, l_send, l_recv, r_send, r_recv, t_send, t_recv, i_sem):
    r = lax.axis_index("row")
    c = lax.axis_index("col")
    z = lax.div(c, 4)
    y = lax.rem(c, 4)
    up = {"y": lax.rem(y + 1, 4), "z": lax.rem(z + 1, 4)}
    down = {"y": lax.rem(y + 3, 4), "z": lax.rem(z + 3, 4)}
    to = {
        ("y", 0): (r, z * 4 + up["y"]),
        ("y", 1): (r, z * 4 + down["y"]),
        ("z", 0): (r, up["z"] * 4 + y),
        ("z", 1): (r, down["z"] * 4 + y),
        ("x", 0): (lax.rem(r + 2, NR), c),
        ("x", 1): (lax.rem(r + 6, NR), c),
        "core": (r + 1 - 2 * lax.rem(r, 2), c),
    }
    r_up, r_down, r_far = lax.rem(r + 2, NR), lax.rem(r + 6, NR), lax.rem(r + 4, NR)

    barrier = pltpu.get_barrier_semaphore()
    for target in to.values():
        pl.semaphore_signal(barrier, inc=1, device_id=target, device_id_type=MESH)

    def drain(ref, sem):
        pltpu.make_async_copy(ref, ref, sem).wait()

    def send(ref, target, send_sem, recv_sem):
        pltpu.make_async_remote_copy(
            src_ref=ref, dst_ref=ref, send_sem=send_sem, recv_sem=recv_sem, device_id=target, device_id_type=MESH
        ).start()

    left = {"S": ls, "D": ld}
    right = {"S": rs, "Q": rq, "D": rd, "W": rw}

    def left_step(stage, x, p):
        buf, h, a = left[x], HALF[p], OFFS[p]
        n = "SD".index(x) * NP + p
        out = l_send.at[n]
        both = pl.ds(a, 2 * h)
        one, two = pl.ds(a, h), pl.ds(a + h, h)
        ones = (pl.ds(a, h // 2), pl.ds(a + h // 2, h // 2))
        twos = (pl.ds(a + h, h // 2), pl.ds(a + h + h // 2, h // 2))
        backs = (down, up)
        far_y, far_z = lax.rem(y + 2, 4), lax.rem(z + 2, 4)
        if stage == "a":
            for axis in "yz":
                for side in (0, 1):
                    send(buf.at[z, y, both], to[axis, side], out, l_recv.at[4 * n])
        elif stage == "b":
            drain(buf.at[0, :, both], l_recv.at[4 * n])
            for side in (0, 1):
                send(buf.at[z, backs[side]["y"], ones[side]], to["y", side], out, l_recv.at[4 * n + 1])
                send(buf.at[backs[side]["z"], y, twos[side]], to["z", side], out, l_recv.at[4 * n + 1])
            for back in backs:
                for side in (0, 1):
                    send(buf.at[z, back["y"], one], to["z", side], out, l_recv.at[4 * n + 2])
                    send(buf.at[back["z"], y, two], to["y", side], out, l_recv.at[4 * n + 2])
        elif stage == "c":
            drain(buf.at[0, 0, both], l_recv.at[4 * n + 1])
            for side in (0, 1):
                send(buf.at[z, far_y, one], to["z", side], out, l_recv.at[4 * n + 2])
                send(buf.at[far_z, y, two], to["y", side], out, l_recv.at[4 * n + 2])
        elif stage == "d":
            drain(buf.at[pl.ds(0, 3), :, one], l_recv.at[4 * n + 2])
            for side in (0, 1):
                send(buf.at[backs[side]["z"], :, ones[side]], to["z", side], out, l_recv.at[4 * n + 3])
                send(buf.at[:, backs[side]["y"], twos[side]], to["y", side], out, l_recv.at[4 * n + 3])
        else:
            drain(buf.at[0, :, both], l_recv.at[4 * n + 3])

    def right_step(stage, x, p):
        buf, a, n = right[x], OFFS[p], 2 * HALF[p]
        k = "SQDW".index(x) * NP + p
        out, near, far, core = r_send.at[k], r_recv.at[3 * k], r_recv.at[3 * k + 1], r_recv.at[3 * k + 2]
        rows = pl.ds(a, n)
        if stage == "a":
            send(buf.at[r, rows], to["x", 0], out, near)
            send(buf.at[r, rows], to["x", 1], out, near)
            send(buf.at[r, rows], to["core"], out, core)
        elif stage == "b":
            drain(buf.at[pl.ds(0, 2), rows], near)
            send(buf.at[r_down, pl.ds(a, n // 2)], to["x", 0], out, far)
            send(buf.at[r_up, pl.ds(a + n // 2, n // 2)], to["x", 1], out, far)
            send(buf.at[r_down, rows], to["core"], out, core)
            send(buf.at[r_up, rows], to["core"], out, core)
        elif stage == "c":
            drain(buf.at[0, rows], far)
            send(buf.at[r_far, rows], to["core"], out, core)
        else:
            drain(buf.at[pl.ds(0, 4), rows], core)

    def all_sent():
        for n in range(2 * NP):
            drain(ls.at[pl.ds(0, 3), pl.ds(0, 2), pl.ds(0, 5 * HALF[n % NP])], l_send.at[n])
        for k in range(4 * NP):
            drain(rs.at[pl.ds(0, 7), pl.ds(0, 2 * HALF[k % NP])], r_send.at[k])

    def whole(buf, panel, a, n):
        rows = pl.ds(a, n)
        acc[rows, :] = jnp.zeros((n, COLS), F32)

        def step(i, _):
            lhs = jnp.concatenate([buf[i, j, rows, :] for j in range(4)], axis=1)
            rhs = panel[pl.ds(2 * i, 2)].reshape(4 * COLS, COLS)
            acc[rows, :] += jnp.dot(lhs, rhs, preferred_element_type=F32)
            return 0

        lax.fori_loop(0, 4, step, 0)

    def part(buf, panel, a, n, q):
        rows = pl.ds(a, n)
        lo, size = PART[q]
        group = 1024 // size

        def piece(i, j):
            zz = i * (group // 2) + j // 2
            cols = []
            for half in (0, 1):
                s, e = max(lo, half * COLS), min(lo + size, (half + 1) * COLS)
                if s < e:
                    cols.append(buf[zz, 2 * (j % 2) + half, rows, s - half * COLS : e - half * COLS])
            return cols

        def step(i, _):
            lhs = jnp.concatenate([v for j in range(group) for v in piece(i, j)], axis=1)
            rhs = panel[pl.ds(group * i, group), pl.ds(lo, size), :].reshape(1024, COLS)
            acc[rows, :] += jnp.dot(lhs, rhs, preferred_element_type=F32)
            return 0

        if q == 0:
            acc[rows, :] = jnp.zeros((n, COLS), F32)
        if NR == group:
            step(0, 0)
        else:
            lax.fori_loop(0, NR // group, step, 0)

    def fetch(i):
        return pltpu.make_async_copy((ham, deriv)[i], fetched.at[i], i_sem.at[i])

    def split(buf, panel, early):
        h = HALF[LAST]
        one, two = pl.ds(OFFS[LAST], h), pl.ds(OFFS[LAST] + h, h)
        if early:
            acc[pl.ds(OFFS[LAST], 2 * h), :] = jnp.zeros((2 * h, COLS), F32)

        def step(i, _):
            zz = lax.rem(z + i + lax.div(i, 2), 4) if early else lax.rem(z + 2, 4)
            yy = lax.rem(y + i + lax.div(i, 2), 4) if early else lax.rem(y + 2, 4)
            lhs = jnp.concatenate([buf[zz, j, one, :] for j in range(4)], axis=1)
            rhs = panel[pl.ds(2 * zz, 2)].reshape(4 * COLS, COLS)
            acc[one, :] += jnp.dot(lhs, rhs, preferred_element_type=F32)
            lhs = jnp.concatenate([buf[j, yy, two, :] for j in range(4)], axis=1)
            rows = pl.ds(pl.multiple_of(lax.rem(yy, 2) * COLS, COLS), COLS)
            rhs = jnp.concatenate([panel[2 * j + lax.div(yy, 2), rows, :] for j in range(4)], axis=0)
            acc[two, :] += jnp.dot(lhs, rhs, preferred_element_type=F32)
            return 0

        if early:
            lax.fori_loop(0, 3, step, 0)
        else:
            step(0, 0)

    def begin():
        get_ham = fetch(0)
        get_ham.start()
        fetch(1).start()
        for i in range(6):
            for j in range(3):
                row, col = r * 6 + i, c * 3 + j
                inside = jnp.abs(row - col) <= jnp.maximum(band[row], band[col])
                mask[pl.ds(i * BLK, BLK), pl.ds(j * BLK, BLK)] = jnp.full((BLK, BLK), jnp.where(inside, 1.0, 0.0), F32)
        get_ham.wait()
        start = (fetched[0].astype(F32) * mask[...]).astype(BF16)
        rs[r] = start
        ls[z, y] = start
        mine[...] = jnp.zeros((8, BLK), F32)
        terms[...] = jnp.zeros((8, COLS), F32)
        pl.semaphore_wait(barrier, len(to))

    def prepare():
        line = lax.broadcasted_iota(jnp.int32, (8, BLK), 0)
        for f in (0, 1):
            for k in range(NC):
                tile = jnp.zeros((8, BLK), F32)
                for m in range(3):
                    tile = jnp.where(line == m, jnp.where(frag[3 * k + m] == 2 * c + f, 1.0, 0.0), tile)
                weights[f, k] = tile

    def square_rows(p):
        a, n = OFFS[p], 2 * HALF[p]
        if p == LAST:
            split(ls, rs, False)
        else:
            whole(ls, rs, a, n)
        rq[r, pl.ds(a, n), :] = (acc[pl.ds(a, n), :] * mask[pl.ds(a, n), :]).astype(BF16)

    def density_rows(p):
        a, n = OFFS[p], 2 * HALF[p]
        rows = pl.ds(a, n)
        sign = 1.5 * rs[r, rows, :].astype(F32) - 0.5 * acc[rows, :]
        sign = (mask[rows, :] * sign).astype(BF16)
        n_out[rows, :] = sign
        line = r * ROWS + a + lax.broadcasted_iota(jnp.int32, (n, COLS), 0)
        column = c * COLS + lax.broadcasted_iota(jnp.int32, (n, COLS), 1)
        identity = jnp.where(line == column, 1.0, 0.0)
        density = (0.5 * (identity - sign.astype(F32))).astype(BF16)
        rd[r, rows, :] = density
        ld[z, y, rows, :] = density

    def weighted_rows(u):
        rows = pl.ds(256 * u, 256)
        rw[r, rows, :] = (acc[rows, :] * mask[rows, :]).astype(BF16)

    def energy_rows(p):
        a, n = OFFS[p], 2 * HALF[p]
        rows = pl.ds(a, n)
        if p == FIRST:
            fetch(1).wait()
        energy = (acc[rows, :] * mask[rows, :]).astype(BF16)
        e_out[rows, :] = energy
        product = energy.astype(F32) * fetched[1, rows, :].astype(F32)
        terms[...] += jnp.sum(product.reshape(n // 8, 8, COLS), axis=0)

    def finish():
        total = jnp.sum(terms[...], axis=0, keepdims=True)
        for m in range(3):
            mine[pl.ds(m, 1), :] = total[:, m * BLK : (m + 1) * BLK]
        by_row[r] = mine[...]
        for k in range(1, NR):
            pltpu.make_async_remote_copy(
                src_ref=mine, dst_ref=by_row.at[r], send_sem=t_send.at[0], recv_sem=t_recv.at[0],
                device_id=(lax.rem(r + k, NR), c), device_id_type=MESH,
            ).start()
        drain(by_row.at[pl.ds(0, NR - 1)], t_recv.at[0])
        by_col[c] = jnp.sum(by_row[...], axis=0)
        for k in range(1, NC):
            send(by_col.at[c], (r, lax.rem(c + k, NC)), t_send.at[1], t_recv.at[1])
        all_sent()
        drain(by_row.at[pl.ds(0, NR - 1)], t_send.at[0])
        drain(by_col.at[pl.ds(0, NC - 1)], t_recv.at[1])
        for f in (0, 1):
            picked = jnp.sum(weights[f] * by_col[...], axis=0)
            pulay[pl.ds(f, 1), :] = jnp.sum(picked, axis=0, keepdims=True)
        drain(by_col.at[pl.ds(0, NC - 1)], t_send.at[1])

    begin()
    for name in ORDER:
        digits = [int(d) for d in name if d.isdigit()]
        if name[0] == "L":
            left_step(name[1], name[2], digits[0])
        elif name[0] == "R":
            right_step(name[1], name[2], digits[0])
        elif name[:3] in ("P1e", "P4e"):
            split(*((ls, rs) if name[1] == "1" else (ld, rw)), True)
        elif name[:2] == "P1":
            square_rows(digits[1])
        elif name[:2] in ("P2", "P3"):
            part(ls, rq if name[1] == "2" else rd, 256 * digits[1], 256, digits[2])
        elif name[:2] == "P4":
            p = digits[1]
            if len(digits) == 3:
                part(ld, rw, OFFS[p], 2 * HALF[p], digits[2])
            elif p == LAST:
                split(ld, rw, False)
            else:
                whole(ld, rw, OFFS[p], 2 * HALF[p])
        elif name[0] == "N":
            density_rows(digits[0])
        elif name[0] == "W":
            weighted_rows(digits[0])
        elif name[0] == "E":
            energy_rows(digits[0])
        else:
            prepare()
    finish()


def write_out(n_in, e_in, p_in, n_out, e_out, p_out, sems):
    copies = [
        pltpu.make_async_copy(src, dst, sems.at[i])
        for i, (src, dst) in enumerate(((n_in, n_out), (e_in, e_out), (p_in, p_out)))
    ]
    for copy in copies:
        copy.start()
    for copy in copies:
        copy.wait()


def step(ham, deriv, band, frag_of):
    vmem = pl.BlockSpec(memory_space=pltpu.VMEM)
    smem = pl.BlockSpec(memory_space=pltpu.SMEM)
    hbm = pl.BlockSpec(memory_space=pl.ANY)
    dma = pltpu.SemaphoreType.DMA
    panel = pltpu.VMEM((NR, ROWS, COLS), BF16)
    slab = pltpu.VMEM((4, 4, ROWS, COLS), BF16)
    shapes = (((ROWS, COLS), BF16), ((ROWS, COLS), BF16), ((2, BLK), F32))
    held = pl.pallas_call(
        kernel,
        out_shape=tuple(pltpu.VMEM(*shape) for shape in shapes),
        in_specs=[smem, smem, hbm, hbm],
        out_specs=(vmem, vmem, vmem),
        scratch_shapes=[
            slab, slab, panel, panel, panel, panel,
            pltpu.VMEM((ROWS, COLS), F32),
            pltpu.VMEM((ROWS, COLS), F32),
            pltpu.VMEM((8, COLS), F32),
            pltpu.VMEM((8, BLK), F32),
            pltpu.VMEM((NR, 8, BLK), F32),
            pltpu.VMEM((NC, 8, BLK), F32),
            pltpu.VMEM((2, NC, 8, BLK), F32),
            pltpu.VMEM((2, ROWS, COLS), BF16),
            dma((2 * NP,)), dma((8 * NP,)), dma((4 * NP,)), dma((12 * NP,)), dma((2,)), dma((2,)), dma((2,)),
        ],
        compiler_params=pltpu.CompilerParams(collective_id=0, has_side_effects=True, vmem_limit_bytes=56 << 20),
        name="sign_step",
    )(band, frag_of, ham, deriv)
    return pl.pallas_call(
        write_out,
        out_shape=tuple(jax.ShapeDtypeStruct(*shape) for shape in shapes),
        in_specs=[vmem, vmem, vmem],
        out_specs=(hbm, hbm, hbm),
        scratch_shapes=[dma((3,))],
        name="write_out",
    )(*(pltpu.with_memory_space_constraint(x, pltpu.VMEM) for x in held))


def solution(mesh):
    return jax.shard_map(
        step,
        mesh=mesh,
        in_specs=(P("row", "col"), P("row", "col"), P(), P()),
        out_specs=(P("row", "col"), P("row", "col"), P("col", None)),
        check_vma=False,
    )
```

```python
import functools

import jax
import jax.numpy as jnp
from jax import lax
from jax.experimental import pallas as pl
from jax.experimental.pallas import tpu as pltpu
from jax.sharding import PartitionSpec as P

MESH = pl.DeviceIdType.MESH
BLK = 128
ROWS = 768
COLS = 384
NR = 8
NC = 16
F32 = jnp.float32
BF16 = jnp.bfloat16
OFFS = (0, 256, 512, 640)
HALF = (128, 128, 64, 64)
NP = len(HALF)
LAST = NP - 1
PART = ((0, 256), (256, 256), (512, 128), (640, 128))
ORDER = (
    "RaS0", "LaS1", "LaS0", "prep", "RaS1", "RbS0", "LbS1", "LxS1", "RbS1", "LbS0", "LxS0", "LcS1",
    "RcS0", "RdS0", "RcS1", "RaS2", "RdS1", "LcS0", "LaS2", "RbS2", "RcS2", "RaS3", "RdS2", "LdS1",
    "LdS0", "LaS3", "RbS3", "LbS2", "LxS2", "RcS3", "RdS3", "LeS1", "P1_1", "RaQ1", "LeS0", "P1_0",
    "RaQ0", "LbS3", "LcS2", "LxS3", "RbQ1", "LcS3", "LdS2", "RbQ0", "LdS3", "P1e_3", "RcQ1", "LeS2",
    "P1_2", "RcQ0", "RaQ2", "RdQ1", "LeS3", "P1_3", "RaQ3", "RdQ0", "P2_00", "P2_01", "P2_20", "P2_21",
    "RbQ2", "P2_10", "P2_11", "RbQ3", "RcQ2", "RdQ2", "P2_02", "P2_22", "RcQ3", "P2_12", "RdQ3", "P2_03",
    "N0", "RaD0", "LaD0", "P2_13", "N1", "RaD1", "LaD1", "P2_23", "N2", "RaD2", "N3", "RaD3",
    "LaD3", "RbD0", "LbD0", "LxD0", "RbD1", "LbD1", "LxD1", "RbD2", "LcD0", "RbD3", "RcD0", "RdD0",
    "P3_20", "LcD1", "LaD2", "RcD1", "P3_00", "RcD2", "P3_10", "RdD1", "RcD3", "P3_01", "RdD2", "P3_02",
    "RdD3", "P3_03", "W0", "RaW0", "P3_11", "P3_12", "P3_13", "W1", "RaW1", "P3_21", "P3_22", "P3_23",
    "W2", "RaW2", "LdD0", "LdD1", "RbW0", "RaW3", "LbD2", "LbD3", "LxD2", "RbW1", "LeD0", "RbW2",
    "RcW0", "LeD1", "LcD2", "LxD3", "RdW0", "P4_10", "LcD3", "P4_00", "RbW3", "RcW1", "LdD2", "RcW2",
    "RdW1", "P4_01", "RdW2", "RcW3", "P4_11", "P4_12", "LdD3", "RdW3", "P4e_3", "P4_13", "E1", "LeD2",
    "P4_2", "E2", "P4_02", "P4_03", "LeD3", "P4_3", "E3", "E0",
)
FIRST = next(int(name[1]) for name in ORDER if name[0] == "E")


def kernel(band, frag, ham, deriv, n_out, e_out, pulay, ls, ld, rs, rq, rd, rw, mask, acc, terms, mine, by_row, by_col,
           weights, fetched, l_send, l_recv, r_send, r_recv, t_send, t_recv, i_sem):
    r = lax.axis_index("row")
    c = lax.axis_index("col")
    z = lax.div(c, 4)
    y = lax.rem(c, 4)
    up = {"y": lax.rem(y + 1, 4), "z": lax.rem(z + 1, 4)}
    down = {"y": lax.rem(y + 3, 4), "z": lax.rem(z + 3, 4)}
    to = {
        ("y", 0): (r, z * 4 + up["y"]),
        ("y", 1): (r, z * 4 + down["y"]),
        ("z", 0): (r, up["z"] * 4 + y),
        ("z", 1): (r, down["z"] * 4 + y),
        ("x", 0): (lax.rem(r + 2, NR), c),
        ("x", 1): (lax.rem(r + 6, NR), c),
        "core": (r + 1 - 2 * lax.rem(r, 2), c),
    }
    r_up, r_down, r_far = lax.rem(r + 2, NR), lax.rem(r + 6, NR), lax.rem(r + 4, NR)

    barrier = pltpu.get_barrier_semaphore()
    for target in to.values():
        pl.semaphore_signal(barrier, inc=1, device_id=target, device_id_type=MESH)

    def drain(ref, sem):
        pltpu.make_async_copy(ref, ref, sem).wait()

    def send(ref, target, send_sem, recv_sem):
        pltpu.make_async_remote_copy(
            src_ref=ref, dst_ref=ref, send_sem=send_sem, recv_sem=recv_sem, device_id=target, device_id_type=MESH
        ).start()

    left = {"S": ls, "D": ld}
    right = {"S": rs, "Q": rq, "D": rd, "W": rw}

    def left_step(stage, x, p):
        buf, h, a = left[x], HALF[p], OFFS[p]
        out = l_send.at[p]
        both = pl.ds(a, 2 * h)
        one, two = pl.ds(a, h), pl.ds(a + h, h)
        ones = (pl.ds(a, h // 2), pl.ds(a + h // 2, h // 2))
        twos = (pl.ds(a + h, h // 2), pl.ds(a + h + h // 2, h // 2))
        backs = (down, up)
        far_y, far_z = lax.rem(y + 2, 4), lax.rem(z + 2, 4)
        if stage == "a":
            for axis in "yz":
                for side in (0, 1):
                    send(buf.at[z, y, both], to[axis, side], out, l_recv.at[4 * p])
        elif stage == "b":
            drain(buf.at[0, :, both], l_recv.at[4 * p])
            for side in (0, 1):
                send(buf.at[z, backs[side]["y"], ones[side]], to["y", side], out, l_recv.at[4 * p + 1])
                send(buf.at[backs[side]["z"], y, twos[side]], to["z", side], out, l_recv.at[4 * p + 1])
        elif stage == "x":
            for back in backs:
                for side in (0, 1):
                    send(buf.at[z, back["y"], one], to["z", side], out, l_recv.at[4 * p + 2])
                    send(buf.at[back["z"], y, two], to["y", side], out, l_recv.at[4 * p + 2])
        elif stage == "c":
            drain(buf.at[0, 0, both], l_recv.at[4 * p + 1])
            for side in (0, 1):
                send(buf.at[z, far_y, one], to["z", side], out, l_recv.at[4 * p + 2])
                send(buf.at[far_z, y, two], to["y", side], out, l_recv.at[4 * p + 2])
        elif stage == "d":
            drain(buf.at[pl.ds(0, 3), :, one], l_recv.at[4 * p + 2])
            for side in (0, 1):
                send(buf.at[backs[side]["z"], :, ones[side]], to["z", side], out, l_recv.at[4 * p + 3])
                send(buf.at[:, backs[side]["y"], twos[side]], to["y", side], out, l_recv.at[4 * p + 3])
        else:
            drain(buf.at[0, :, both], l_recv.at[4 * p + 3])

    def right_step(stage, x, p):
        buf, a, n = right[x], OFFS[p], 2 * HALF[p]
        out, near, far = r_send.at[p], r_recv.at[p], r_recv.at[NP + p]
        core = r_recv.at[2 * NP + 2 * p + "SQDW".index(x) % 2]
        rows = pl.ds(a, n)
        if stage == "a":
            send(buf.at[r, rows], to["x", 0], out, near)
            send(buf.at[r, rows], to["x", 1], out, near)
            send(buf.at[r, rows], to["core"], out, core)
        elif stage == "b":
            drain(buf.at[pl.ds(0, 2), rows], near)
            send(buf.at[r_down, pl.ds(a, n // 2)], to["x", 0], out, far)
            send(buf.at[r_up, pl.ds(a + n // 2, n // 2)], to["x", 1], out, far)
            send(buf.at[r_down, rows], to["core"], out, core)
            send(buf.at[r_up, rows], to["core"], out, core)
        elif stage == "c":
            drain(buf.at[0, rows], far)
            send(buf.at[r_far, rows], to["core"], out, core)
        else:
            drain(buf.at[pl.ds(0, 4), rows], core)

    def all_sent():
        for p in range(NP):
            drain(ls.at[pl.ds(0, 3), :, pl.ds(0, 5 * HALF[p])], l_send.at[p])
            drain(ls.at[:, :, pl.ds(0, 7 * HALF[p] // 2)], r_send.at[p])

    def whole(buf, panel, a, n):
        rows = pl.ds(a, n)
        acc[rows, :] = jnp.zeros((n, COLS), F32)

        def step(i, _):
            lhs = jnp.concatenate([buf[i, j, rows, :] for j in range(4)], axis=1)
            rhs = panel[pl.ds(2 * i, 2)].reshape(4 * COLS, COLS)
            acc[rows, :] += jnp.dot(lhs, rhs, preferred_element_type=F32)
            return 0

        lax.fori_loop(0, 4, step, 0)

    def part(buf, panel, a, n, q):
        rows = pl.ds(a, n)
        lo, size = PART[q]
        group = 1024 // size

        def piece(i, j):
            zz = i * (group // 2) + j // 2
            cols = []
            for half in (0, 1):
                s, e = max(lo, half * COLS), min(lo + size, (half + 1) * COLS)
                if s < e:
                    cols.append(buf[zz, 2 * (j % 2) + half, rows, s - half * COLS : e - half * COLS])
            return cols

        def step(i, _):
            lhs = jnp.concatenate([v for j in range(group) for v in piece(i, j)], axis=1)
            rhs = panel[pl.ds(group * i, group), pl.ds(lo, size), :].reshape(1024, COLS)
            acc[rows, :] += jnp.dot(lhs, rhs, preferred_element_type=F32)
            return 0

        if q == 0:
            acc[rows, :] = jnp.zeros((n, COLS), F32)
        if NR == group:
            step(0, 0)
        else:
            lax.fori_loop(0, NR // group, step, 0)

    def fetch(i):
        return pltpu.make_async_copy((ham, deriv)[i], fetched.at[i], i_sem.at[i])

    def split(buf, panel, early):
        h = HALF[LAST]
        one, two = pl.ds(OFFS[LAST], h), pl.ds(OFFS[LAST] + h, h)
        if early:
            acc[pl.ds(OFFS[LAST], 2 * h), :] = jnp.zeros((2 * h, COLS), F32)

        def step(i, _):
            zz = lax.rem(z + i + lax.div(i, 2), 4) if early else lax.rem(z + 2, 4)
            yy = lax.rem(y + i + lax.div(i, 2), 4) if early else lax.rem(y + 2, 4)
            lhs = jnp.concatenate([buf[zz, j, one, :] for j in range(4)], axis=1)
            rhs = panel[pl.ds(2 * zz, 2)].reshape(4 * COLS, COLS)
            acc[one, :] += jnp.dot(lhs, rhs, preferred_element_type=F32)
            lhs = jnp.concatenate([buf[j, yy, two, :] for j in range(4)], axis=1)
            rows = pl.ds(pl.multiple_of(lax.rem(yy, 2) * COLS, COLS), COLS)
            rhs = jnp.concatenate([panel[2 * j + lax.div(yy, 2), rows, :] for j in range(4)], axis=0)
            acc[two, :] += jnp.dot(lhs, rhs, preferred_element_type=F32)
            return 0

        if early:
            lax.fori_loop(0, 3, step, 0)
        else:
            step(0, 0)

    def begin():
        get_ham = fetch(0)
        get_ham.start()
        fetch(1).start()
        for i in range(6):
            for j in range(3):
                row, col = r * 6 + i, c * 3 + j
                inside = jnp.abs(row - col) <= jnp.maximum(band[row], band[col])
                mask[pl.ds(i * BLK, BLK), pl.ds(j * BLK, BLK)] = jnp.full((BLK, BLK), jnp.where(inside, 1.0, 0.0), F32)
        get_ham.wait()
        start = (fetched[0].astype(F32) * mask[...]).astype(BF16)
        rs[r] = start
        ls[z, y] = start
        mine[...] = jnp.zeros((8, BLK), F32)
        terms[...] = jnp.zeros((8, COLS), F32)
        pl.semaphore_wait(barrier, len(to))

    def prepare():
        line = lax.broadcasted_iota(jnp.int32, (8, BLK), 0)
        for f in (0, 1):
            for k in range(NC):
                tile = jnp.zeros((8, BLK), F32)
                for m in range(3):
                    tile = jnp.where(line == m, jnp.where(frag[3 * k + m] == 2 * c + f, 1.0, 0.0), tile)
                weights[f, k] = tile

    def square_rows(p):
        a, n = OFFS[p], 2 * HALF[p]
        if p == LAST:
            split(ls, rs, False)
        else:
            whole(ls, rs, a, n)
        rq[r, pl.ds(a, n), :] = (acc[pl.ds(a, n), :] * mask[pl.ds(a, n), :]).astype(BF16)

    def density_rows(p):
        a, n = OFFS[p], 2 * HALF[p]
        rows = pl.ds(a, n)
        sign = 1.5 * rs[r, rows, :].astype(F32) - 0.5 * acc[rows, :]
        sign = (mask[rows, :] * sign).astype(BF16)
        n_out[rows, :] = sign
        line = r * ROWS + a + lax.broadcasted_iota(jnp.int32, (n, COLS), 0)
        column = c * COLS + lax.broadcasted_iota(jnp.int32, (n, COLS), 1)
        identity = jnp.where(line == column, 1.0, 0.0)
        density = (0.5 * (identity - sign.astype(F32))).astype(BF16)
        rd[r, rows, :] = density
        ld[z, y, rows, :] = density

    def weighted_rows(u):
        rows = pl.ds(256 * u, 256)
        rw[r, rows, :] = (acc[rows, :] * mask[rows, :]).astype(BF16)

    def energy_rows(p):
        a, n = OFFS[p], 2 * HALF[p]
        rows = pl.ds(a, n)
        if p == FIRST:
            fetch(1).wait()
        energy = (acc[rows, :] * mask[rows, :]).astype(BF16)
        e_out[rows, :] = energy
        product = energy.astype(F32) * fetched[1, rows, :].astype(F32)
        terms[...] += jnp.sum(product.reshape(n // 8, 8, COLS), axis=0)

    def finish():
        total = jnp.sum(terms[...], axis=0, keepdims=True)
        for m in range(3):
            mine[pl.ds(m, 1), :] = total[:, m * BLK : (m + 1) * BLK]
        by_row[r] = mine[...]
        for k in range(1, NR):
            pltpu.make_async_remote_copy(
                src_ref=mine, dst_ref=by_row.at[r], send_sem=t_send.at[0], recv_sem=t_recv.at[0],
                device_id=(lax.rem(r + k, NR), c), device_id_type=MESH,
            ).start()
        drain(by_row.at[pl.ds(0, NR - 1)], t_recv.at[0])
        by_col[c] = jnp.sum(by_row[...], axis=0)
        for k in range(1, NC):
            send(by_col.at[c], (r, lax.rem(c + k, NC)), t_send.at[1], t_recv.at[1])
        all_sent()
        drain(by_row.at[pl.ds(0, NR - 1)], t_send.at[0])
        drain(by_col.at[pl.ds(0, NC - 1)], t_recv.at[1])
        for f in (0, 1):
            picked = jnp.sum(weights[f] * by_col[...], axis=0)
            pulay[pl.ds(f, 1), :] = jnp.sum(picked, axis=0, keepdims=True)
        drain(by_col.at[pl.ds(0, NC - 1)], t_send.at[1])

    begin()
    for name in ORDER:
        digits = [int(d) for d in name if d.isdigit()]
        if name[0] == "L":
            left_step(name[1], name[2], digits[0])
        elif name[0] == "R":
            right_step(name[1], name[2], digits[0])
        elif name[:3] in ("P1e", "P4e"):
            split(*((ls, rs) if name[1] == "1" else (ld, rw)), True)
        elif name[:2] == "P1":
            square_rows(digits[1])
        elif name[:2] in ("P2", "P3"):
            part(ls, rq if name[1] == "2" else rd, 256 * digits[1], 256, digits[2])
        elif name[:2] == "P4":
            p = digits[1]
            if len(digits) == 3:
                part(ld, rw, OFFS[p], 2 * HALF[p], digits[2])
            elif p == LAST:
                split(ld, rw, False)
            else:
                whole(ld, rw, OFFS[p], 2 * HALF[p])
        elif name[0] == "N":
            density_rows(digits[0])
        elif name[0] == "W":
            weighted_rows(digits[0])
        elif name[0] == "E":
            energy_rows(digits[0])
        else:
            prepare()
    finish()


def write_out(n_in, e_in, p_in, n_out, e_out, p_out, sems):
    copies = [
        pltpu.make_async_copy(src, dst, sems.at[i])
        for i, (src, dst) in enumerate(((n_in, n_out), (e_in, e_out), (p_in, p_out)))
    ]
    for copy in copies:
        copy.start()
    for copy in copies:
        copy.wait()


def step(ham, deriv, band, frag_of):
    vmem = pl.BlockSpec(memory_space=pltpu.VMEM)
    smem = pl.BlockSpec(memory_space=pltpu.SMEM)
    hbm = pl.BlockSpec(memory_space=pl.ANY)
    dma = pltpu.SemaphoreType.DMA
    panel = pltpu.VMEM((NR, ROWS, COLS), BF16)
    slab = pltpu.VMEM((4, 4, ROWS, COLS), BF16)
    shapes = (((ROWS, COLS), BF16), ((ROWS, COLS), BF16), ((2, BLK), F32))
    held = pl.pallas_call(
        kernel,
        out_shape=tuple(pltpu.VMEM(*shape) for shape in shapes),
        in_specs=[smem, smem, hbm, hbm],
        out_specs=(vmem, vmem, vmem),
        scratch_shapes=[
            slab, slab, panel, panel, panel, panel,
            pltpu.VMEM((ROWS, COLS), F32),
            pltpu.VMEM((ROWS, COLS), F32),
            pltpu.VMEM((8, COLS), F32),
            pltpu.VMEM((8, BLK), F32),
            pltpu.VMEM((NR, 8, BLK), F32),
            pltpu.VMEM((NC, 8, BLK), F32),
            pltpu.VMEM((2, NC, 8, BLK), F32),
            pltpu.VMEM((2, ROWS, COLS), BF16),
            dma((NP,)), dma((4 * NP,)), dma((NP,)), dma((4 * NP,)), dma((2,)), dma((2,)), dma((2,)),
        ],
        compiler_params=pltpu.CompilerParams(collective_id=0, has_side_effects=True, vmem_limit_bytes=56 << 20),
        name="sign_step",
    )(band, frag_of, ham, deriv)
    return pl.pallas_call(
        write_out,
        out_shape=tuple(jax.ShapeDtypeStruct(*shape) for shape in shapes),
        in_specs=[vmem, vmem, vmem],
        out_specs=(hbm, hbm, hbm),
        scratch_shapes=[dma((3,))],
        name="write_out",
    )(*(pltpu.with_memory_space_constraint(x, pltpu.VMEM) for x in held))


def solution(mesh):
    return jax.shard_map(
        step,
        mesh=mesh,
        in_specs=(P("row", "col"), P("row", "col"), P(), P()),
        out_specs=(P("row", "col"), P("row", "col"), P("col", None)),
        check_vma=False,
    )
```

```python
import functools

import jax
import jax.numpy as jnp
from jax import lax
from jax.experimental import pallas as pl
from jax.experimental.pallas import tpu as pltpu
from jax.sharding import PartitionSpec as P

MESH = pl.DeviceIdType.MESH
BLK = 128
ROWS = 768
COLS = 384
NR = 8
NC = 16
F32 = jnp.float32
BF16 = jnp.bfloat16
OFFS = (0, 256, 512, 640)
HALF = (128, 128, 64, 64)
NP = len(HALF)
PIECES = ((0, 256), (256, 128), (384, 128), (512, 128), (640, 64), (704, 64))
NS = len(PIECES)
LAST = NP - 1
PART = ((0, 256), (256, 256), (512, 128), (640, 128))
ORDER = (
    "LaS3", "RaS1", "LaS0", "prep", "RaS3", "LaS1", "RaS0", "RaS2", "RbS1", "RbS3", "LbS0", "LxS0",
    "RbS0", "LbS1", "RbS2", "RaS5", "LcS0", "LxS1", "RcS1", "LaS2", "RcS3", "RaS4", "RdS1", "RdS3",
    "RcS0", "RcS2", "RdS0", "LcS1", "RbS5", "RdS2", "RbS4", "LdS0", "RcS5", "RcS4", "RdS5", "RdS4",
    "LbS2", "LdS1", "LxS2", "LbS3", "LeS0", "P1_0", "RaQ0", "LcS2", "LxS3", "LeS1", "P1_1", "RaQ1",
    "RaQ2", "LcS3", "LdS2", "RbQ0", "RbQ1", "LdS3", "P1e_3", "RbQ2", "LeS2", "P1_2", "RaQ3", "RcQ0",
    "LeS3", "P1_3", "RaQ5", "RaQ4", "RcQ1", "RdQ0", "P2_10", "P2_20", "RdQ1", "RcQ2", "P2_00", "RbQ3",
    "RdQ2", "P2_01", "RbQ5", "P2_11", "RbQ4", "P2_21", "RcQ3", "RcQ5", "RdQ3", "P2_12", "RcQ4", "P2_02",
    "RdQ5", "P2_22", "RdQ4", "P2_03", "N0", "RaD0", "LaD0", "P2_13", "N1", "RaD1", "LaD1", "RaD2",
    "P2_23", "N2", "LaD2", "RaD3", "N3", "RaD5", "RbD0", "RaD4", "LbD0", "LxD0", "RbD1", "RbD2",
    "LbD1", "LxD1", "RbD3", "RbD5", "LcD0", "LaD3", "RcD0", "RbD4", "RdD0", "P3_10", "RcD1", "P3_20",
    "LcD1", "LbD2", "LxD2", "RcD2", "P3_00", "RdD1", "RcD3", "RdD2", "P3_11", "RcD4", "RcD5", "P3_21",
    "RdD3", "P3_22", "RdD5", "RdD4", "P3_23", "W2", "RaW5", "P3_12", "P3_13", "W1", "RaW2", "P3_01",
    "P3_02", "LdD0", "P3_03", "W0", "RaW0", "RaW1", "RaW3", "RbW5", "LbD3", "RbW2", "LdD1", "LcD2",
    "LxD3", "RbW0", "RaW4", "RbW1", "LeD0", "RbW3", "LcD3", "RcW5", "RcW2", "RdW5", "RdW2", "RcW0",
    "LeD1", "RbW4", "RdW0", "P4_00", "RcW1", "LdD2", "P4_10", "RcW3", "RdW1", "P4_01", "RcW4", "RdW3",
    "P4_02", "LdD3", "P4_11", "P4_12", "RdW4", "P4e_3", "LeD2", "P4_03", "P4_13", "E1", "P4_2", "LeD3",
    "P4_3", "E3", "E2", "E0",
)
FIRST = next(int(name[1]) for name in ORDER if name[0] == "E")


def kernel(band_in, frag_in, ham, deriv, n_out, e_out, pulay, ls, ld, rs, rq, rd, rw, mask, acc, terms, mine, by_row, by_col,
           weights, fetched, band, frag, l_send, l_recv, r_send, r_recv, t_send, t_recv, i_sem):
    r = lax.axis_index("row")
    c = lax.axis_index("col")
    z = lax.div(c, 4)
    y = lax.rem(c, 4)
    up = {"y": lax.rem(y + 1, 4), "z": lax.rem(z + 1, 4)}
    down = {"y": lax.rem(y + 3, 4), "z": lax.rem(z + 3, 4)}
    to = {
        ("y", 0): (r, z * 4 + up["y"]),
        ("y", 1): (r, z * 4 + down["y"]),
        ("z", 0): (r, up["z"] * 4 + y),
        ("z", 1): (r, down["z"] * 4 + y),
        ("x", 0): (lax.rem(r + 2, NR), c),
        ("x", 1): (lax.rem(r + 6, NR), c),
        "core": (r + 1 - 2 * lax.rem(r, 2), c),
    }
    r_up, r_down, r_far = lax.rem(r + 2, NR), lax.rem(r + 6, NR), lax.rem(r + 4, NR)

    barrier = pltpu.get_barrier_semaphore()
    for target in to.values():
        pl.semaphore_signal(barrier, inc=1, device_id=target, device_id_type=MESH)

    def drain(ref, sem):
        pltpu.make_async_copy(ref, ref, sem).wait()

    def send(ref, target, send_sem, recv_sem):
        pltpu.make_async_remote_copy(
            src_ref=ref, dst_ref=ref, send_sem=send_sem, recv_sem=recv_sem, device_id=target, device_id_type=MESH
        ).start()

    left = {"S": ls, "D": ld}
    right = {"S": rs, "Q": rq, "D": rd, "W": rw}

    def left_step(stage, x, p):
        buf, h, a = left[x], HALF[p], OFFS[p]
        out = l_send.at[p]
        both = pl.ds(a, 2 * h)
        one, two = pl.ds(a, h), pl.ds(a + h, h)
        ones = (pl.ds(a, h // 2), pl.ds(a + h // 2, h // 2))
        twos = (pl.ds(a + h, h // 2), pl.ds(a + h + h // 2, h // 2))
        backs = (down, up)
        far_y, far_z = lax.rem(y + 2, 4), lax.rem(z + 2, 4)
        if stage == "a":
            if x == "S":
                start_rows(a, 2 * h)
            for axis in "yz":
                for side in (0, 1):
                    send(buf.at[z, y, both], to[axis, side], out, l_recv.at[4 * p])
        elif stage == "b":
            drain(buf.at[0, :, both], l_recv.at[4 * p])
            for side in (0, 1):
                send(buf.at[z, backs[side]["y"], ones[side]], to["y", side], out, l_recv.at[4 * p + 1])
                send(buf.at[backs[side]["z"], y, twos[side]], to["z", side], out, l_recv.at[4 * p + 1])
        elif stage == "x":
            for back in backs:
                for side in (0, 1):
                    send(buf.at[z, back["y"], one], to["z", side], out, l_recv.at[4 * p + 2])
                    send(buf.at[back["z"], y, two], to["y", side], out, l_recv.at[4 * p + 2])
        elif stage == "c":
            drain(buf.at[0, 0, both], l_recv.at[4 * p + 1])
            for side in (0, 1):
                send(buf.at[z, far_y, one], to["z", side], out, l_recv.at[4 * p + 2])
                send(buf.at[far_z, y, two], to["y", side], out, l_recv.at[4 * p + 2])
        elif stage == "d":
            drain(buf.at[pl.ds(0, 3), :, one], l_recv.at[4 * p + 2])
            for side in (0, 1):
                send(buf.at[backs[side]["z"], :, ones[side]], to["z", side], out, l_recv.at[4 * p + 3])
                send(buf.at[:, backs[side]["y"], twos[side]], to["y", side], out, l_recv.at[4 * p + 3])
        else:
            drain(buf.at[0, :, both], l_recv.at[4 * p + 3])

    def right_step(stage, x, p):
        buf = right[x]
        a, n = PIECES[p]
        out, near, far = r_send.at[p], r_recv.at[p], r_recv.at[NS + p]
        core = r_recv.at[2 * NS + 2 * p + "SQDW".index(x) % 2]
        rows = pl.ds(a, n)
        if stage == "a":
            if x == "S":
                start_rows(a, n)
            send(buf.at[r, rows], to["x", 0], out, near)
            send(buf.at[r, rows], to["x", 1], out, near)
            send(buf.at[r, rows], to["core"], out, core)
        elif stage == "b":
            drain(buf.at[pl.ds(0, 2), rows], near)
            send(buf.at[r_down, pl.ds(a, n // 2)], to["x", 0], out, far)
            send(buf.at[r_up, pl.ds(a + n // 2, n // 2)], to["x", 1], out, far)
            send(buf.at[r_down, rows], to["core"], out, core)
            send(buf.at[r_up, rows], to["core"], out, core)
        elif stage == "c":
            drain(buf.at[0, rows], far)
            send(buf.at[r_far, rows], to["core"], out, core)
        else:
            drain(buf.at[pl.ds(0, 4), rows], core)

    def all_sent():
        for p in range(NP):
            drain(ls.at[pl.ds(0, 3), :, pl.ds(0, 5 * HALF[p])], l_send.at[p])
        for p, (_, n) in enumerate(PIECES):
            drain(ls.at[:, :, pl.ds(0, 7 * n // 4)], r_send.at[p])

    def whole(buf, panel, a, n):
        rows = pl.ds(a, n)
        acc[rows, :] = jnp.zeros((n, COLS), F32)

        def step(i, _):
            lhs = jnp.concatenate([buf[i, j, rows, :] for j in range(4)], axis=1)
            rhs = panel[pl.ds(2 * i, 2)].reshape(4 * COLS, COLS)
            acc[rows, :] += jnp.dot(lhs, rhs, preferred_element_type=F32)
            return 0

        lax.fori_loop(0, 4, step, 0)

    def part(buf, panel, a, n, q):
        rows = pl.ds(a, n)
        lo, size = PART[q]
        group = 1024 // size

        def piece(i, j):
            zz = i * (group // 2) + j // 2
            cols = []
            for half in (0, 1):
                s, e = max(lo, half * COLS), min(lo + size, (half + 1) * COLS)
                if s < e:
                    cols.append(buf[zz, 2 * (j % 2) + half, rows, s - half * COLS : e - half * COLS])
            return cols

        def step(i, _):
            lhs = jnp.concatenate([v for j in range(group) for v in piece(i, j)], axis=1)
            rhs = panel[pl.ds(group * i, group), pl.ds(lo, size), :].reshape(1024, COLS)
            acc[rows, :] += jnp.dot(lhs, rhs, preferred_element_type=F32)
            return 0

        if q == 0:
            acc[rows, :] = jnp.zeros((n, COLS), F32)
        if NR == group:
            step(0, 0)
        else:
            lax.fori_loop(0, NR // group, step, 0)

    def fetch(i):
        if i < 3:
            rows = pl.ds(256 * i, 256)
            return pltpu.make_async_copy(ham.at[rows], fetched.at[0, rows], i_sem.at[i])
        src, dst = ((deriv, fetched.at[1]), (band_in, band), (frag_in, frag))[i - 3]
        return pltpu.make_async_copy(src, dst, i_sem.at[i])

    def split(buf, panel, early):
        h = HALF[LAST]
        one, two = pl.ds(OFFS[LAST], h), pl.ds(OFFS[LAST] + h, h)
        if early:
            acc[pl.ds(OFFS[LAST], 2 * h), :] = jnp.zeros((2 * h, COLS), F32)

        def step(i, _):
            zz = lax.rem(z + i + lax.div(i, 2), 4) if early else lax.rem(z + 2, 4)
            yy = lax.rem(y + i + lax.div(i, 2), 4) if early else lax.rem(y + 2, 4)
            lhs = jnp.concatenate([buf[zz, j, one, :] for j in range(4)], axis=1)
            rhs = panel[pl.ds(2 * zz, 2)].reshape(4 * COLS, COLS)
            acc[one, :] += jnp.dot(lhs, rhs, preferred_element_type=F32)
            lhs = jnp.concatenate([buf[j, yy, two, :] for j in range(4)], axis=1)
            rows = pl.ds(pl.multiple_of(lax.rem(yy, 2) * COLS, COLS), COLS)
            rhs = jnp.concatenate([panel[2 * j + lax.div(yy, 2), rows, :] for j in range(4)], axis=0)
            acc[two, :] += jnp.dot(lhs, rhs, preferred_element_type=F32)
            return 0

        if early:
            lax.fori_loop(0, 3, step, 0)
        else:
            step(0, 0)

    first = int(ORDER[0][3])
    first = (OFFS if ORDER[0][0] == "L" else [a for a, _ in PIECES])[first] // 256
    order_of_rows = (first, *(i for i in range(3) if i != first))
    ready = {}

    def start_rows(a, n):
        for i in range(a // BLK, (a + n + BLK - 1) // BLK):
            if i in ready:
                continue
            if not ready:
                fetch(4).wait()
            if i // 2 not in ready.values():
                fetch(i // 2).wait()
            ready[i] = i // 2
            rows = pl.ds(i * BLK, BLK)
            for j in range(3):
                row, col, cols = r * 6 + i, c * 3 + j, pl.ds(j * BLK, BLK)
                inside = jnp.abs(row - col) <= jnp.maximum(band[row], band[col])
                block = jnp.full((BLK, BLK), jnp.where(inside, 1.0, 0.0), F32)
                mask[rows, cols] = block
                start = (fetched[0, rows, cols].astype(F32) * block).astype(BF16)
                rs[r, rows, cols] = start
                ls[z, y, rows, cols] = start

    def begin():
        for i in (4, *order_of_rows, 5, 3):
            fetch(i).start()
        terms[...] = jnp.zeros((8, COLS), F32)
        start_rows(256 * order_of_rows[0], 256)
        pl.semaphore_wait(barrier, len(to))

    def prepare():
        fetch(5).wait()
        for f in (0, 1):
            for j in range(3 * NC):
                weight = jnp.where(frag[j] == 2 * c + f, 1.0, 0.0)
                weights[f, j // 3, :, pl.ds(j % 3 * BLK, BLK)] = jnp.full((1, BLK), weight, F32)

    def square_rows(p):
        a, n = OFFS[p], 2 * HALF[p]
        if p == LAST:
            split(ls, rs, False)
        else:
            whole(ls, rs, a, n)
        rq[r, pl.ds(a, n), :] = (acc[pl.ds(a, n), :] * mask[pl.ds(a, n), :]).astype(BF16)

    def density_rows(p):
        a, n = OFFS[p], 2 * HALF[p]
        rows = pl.ds(a, n)
        sign = 1.5 * rs[r, rows, :].astype(F32) - 0.5 * acc[rows, :]
        sign = (mask[rows, :] * sign).astype(BF16)
        n_out[rows, :] = sign
        line = r * ROWS + a + lax.broadcasted_iota(jnp.int32, (n, COLS), 0)
        column = c * COLS + lax.broadcasted_iota(jnp.int32, (n, COLS), 1)
        identity = jnp.where(line == column, 1.0, 0.0)
        density = (0.5 * (identity - sign.astype(F32))).astype(BF16)
        rd[r, rows, :] = density
        ld[z, y, rows, :] = density

    def weighted_rows(u):
        rows = pl.ds(256 * u, 256)
        rw[r, rows, :] = (acc[rows, :] * mask[rows, :]).astype(BF16)

    def energy_rows(p):
        a, n = OFFS[p], 2 * HALF[p]
        rows = pl.ds(a, n)
        if p == FIRST:
            fetch(3).wait()
        energy = (acc[rows, :] * mask[rows, :]).astype(BF16)
        e_out[rows, :] = energy
        product = energy.astype(F32) * fetched[1, rows, :].astype(F32)
        terms[...] += jnp.sum(product.reshape(n // 8, 8, COLS), axis=0)

    def finish():
        mine[...] = jnp.sum(terms[...], axis=0, keepdims=True)
        by_row[r] = mine[...]
        for k in range(1, NR):
            pltpu.make_async_remote_copy(
                src_ref=mine, dst_ref=by_row.at[r], send_sem=t_send.at[0], recv_sem=t_recv.at[0],
                device_id=(lax.rem(r + k, NR), c), device_id_type=MESH,
            ).start()
        drain(by_row.at[pl.ds(0, NR - 1)], t_recv.at[0])
        by_col[c] = jnp.sum(by_row[...], axis=0)
        for k in range(1, NC):
            send(by_col.at[c], (r, lax.rem(c + k, NC)), t_send.at[1], t_recv.at[1])
        all_sent()
        drain(by_row.at[pl.ds(0, NR - 1)], t_send.at[0])
        drain(by_col.at[pl.ds(0, NC - 1)], t_recv.at[1])
        for f in (0, 1):
            picked = jnp.sum(weights[f] * by_col[...], axis=0)
            pulay[pl.ds(f, 1), :] = picked[:, :BLK] + picked[:, BLK : 2 * BLK] + picked[:, 2 * BLK :]
        drain(by_col.at[pl.ds(0, NC - 1)], t_send.at[1])

    begin()
    for name in ORDER:
        digits = [int(d) for d in name if d.isdigit()]
        if name[0] == "L":
            left_step(name[1], name[2], digits[0])
        elif name[0] == "R":
            right_step(name[1], name[2], digits[0])
        elif name[:3] in ("P1e", "P4e"):
            split(*((ls, rs) if name[1] == "1" else (ld, rw)), True)
        elif name[:2] == "P1":
            square_rows(digits[1])
        elif name[:2] in ("P2", "P3"):
            part(ls, rq if name[1] == "2" else rd, 256 * digits[1], 256, digits[2])
        elif name[:2] == "P4":
            p = digits[1]
            if len(digits) == 3:
                part(ld, rw, OFFS[p], 2 * HALF[p], digits[2])
            elif p == LAST:
                split(ld, rw, False)
            else:
                whole(ld, rw, OFFS[p], 2 * HALF[p])
        elif name[0] == "N":
            density_rows(digits[0])
        elif name[0] == "W":
            weighted_rows(digits[0])
        elif name[0] == "E":
            energy_rows(digits[0])
        else:
            prepare()
    finish()


def write_out(n_in, e_in, p_in, n_out, e_out, p_out, sems):
    copies = [
        pltpu.make_async_copy(src, dst, sems.at[i])
        for i, (src, dst) in enumerate(((n_in, n_out), (e_in, e_out), (p_in, p_out)))
    ]
    for copy in copies:
        copy.start()
    for copy in copies:
        copy.wait()


def step(ham, deriv, band, frag_of):
    vmem = pl.BlockSpec(memory_space=pltpu.VMEM)
    hbm = pl.BlockSpec(memory_space=pl.ANY)
    dma = pltpu.SemaphoreType.DMA
    panel = pltpu.VMEM((NR, ROWS, COLS), BF16)
    slab = pltpu.VMEM((4, 4, ROWS, COLS), BF16)
    shapes = (((ROWS, COLS), BF16), ((ROWS, COLS), BF16), ((2, BLK), F32))
    held = pl.pallas_call(
        kernel,
        out_shape=tuple(pltpu.VMEM(*shape) for shape in shapes),
        in_specs=[hbm, hbm, hbm, hbm],
        out_specs=(vmem, vmem, vmem),
        scratch_shapes=[
            slab, slab, panel, panel, panel, panel,
            pltpu.VMEM((ROWS, COLS), F32),
            pltpu.VMEM((ROWS, COLS), F32),
            pltpu.VMEM((8, COLS), F32),
            pltpu.VMEM((1, COLS), F32),
            pltpu.VMEM((NR, 1, COLS), F32),
            pltpu.VMEM((NC, 1, COLS), F32),
            pltpu.VMEM((2, NC, 1, COLS), F32),
            pltpu.VMEM((2, ROWS, COLS), BF16),
            pltpu.SMEM((6 * NR,), jnp.int32),
            pltpu.SMEM((6 * NR,), jnp.int32),
            dma((NP,)), dma((4 * NP,)), dma((NS,)), dma((4 * NS,)), dma((2,)), dma((2,)), dma((6,)),
        ],
        compiler_params=pltpu.CompilerParams(collective_id=0, has_side_effects=True, vmem_limit_bytes=56 << 20),
        name="sign_step",
    )(band, frag_of, ham, deriv)
    return pl.pallas_call(
        write_out,
        out_shape=tuple(jax.ShapeDtypeStruct(*shape) for shape in shapes),
        in_specs=[vmem, vmem, vmem],
        out_specs=(hbm, hbm, hbm),
        scratch_shapes=[dma((3,))],
        name="write_out",
    )(*(pltpu.with_memory_space_constraint(x, pltpu.VMEM) for x in held))


def solution(mesh):
    return jax.shard_map(
        step,
        mesh=mesh,
        in_specs=(P("row", "col"), P("row", "col"), P(), P()),
        out_specs=(P("row", "col"), P("row", "col"), P("col", None)),
        check_vma=False,
    )
```

```python
import functools

import jax
import jax.numpy as jnp
from jax import lax
from jax.experimental import pallas as pl
from jax.experimental.pallas import tpu as pltpu
from jax.sharding import PartitionSpec as P

MESH = pl.DeviceIdType.MESH
BLK = 128
ROWS = 768
COLS = 384
NR = 8
NC = 16
F32 = jnp.float32
BF16 = jnp.bfloat16
OFFS = (0, 256, 512, 640)
HALF = (128, 128, 64, 64)
NP = len(HALF)
PIECES = ((0, 256), (256, 128), (384, 128), (512, 128), (640, 64), (704, 64))
NS = len(PIECES)
LAST = NP - 1
PART = ((0, 256), (256, 256), (512, 128), (640, 128))
ORDER = (
    "LaS3", "RaS1", "LaS0", "prep", "RaS3", "LaS1", "RaS0", "RaS2", "RbS1", "RbS3", "LbS0", "LxS0",
    "RbS0", "LbS1", "RbS2", "RaS5", "LcS0", "LxS1", "RcS1", "LaS2", "RcS3", "RaS4", "RdS1", "RdS3",
    "RcS0", "RcS2", "RdS0", "LcS1", "RbS5", "RdS2", "RbS4", "LdS0", "RcS5", "RcS4", "RdS5", "RdS4",
    "LbS2", "LdS1", "LxS2", "LbS3", "LeS0", "P1_0", "RaQ0", "LcS2", "LxS3", "LeS1", "P1_1", "RaQ1",
    "RaQ2", "LcS3", "LdS2", "RbQ0", "RbQ1", "LdS3", "P1e_3", "RbQ2", "LeS2", "P1_2", "RaQ3", "RcQ0",
    "LeS3", "P1_3", "RaQ5", "RaQ4", "RcQ1", "RdQ0", "P2_10", "P2_20", "RdQ1", "RcQ2", "P2_00", "RbQ3",
    "RdQ2", "P2_01", "RbQ5", "P2_11", "RbQ4", "P2_21", "RcQ3", "RcQ5", "RdQ3", "P2_12", "RcQ4", "P2_02",
    "RdQ5", "P2_22", "RdQ4", "P2_03", "N0", "RaD0", "LaD0", "P2_13", "N1", "RaD1", "LaD1", "RaD2",
    "P2_23", "N2", "LaD2", "RaD3", "N3", "RaD5", "RbD0", "RaD4", "LbD0", "LxD0", "RbD1", "RbD2",
    "LbD1", "LxD1", "RbD3", "RbD5", "LcD0", "LaD3", "RcD0", "RbD4", "RdD0", "P3_10", "RcD1", "P3_20",
    "LcD1", "LbD2", "LxD2", "RcD2", "P3_00", "RdD1", "RcD3", "RdD2", "P3_11", "RcD4", "RcD5", "P3_21",
    "RdD3", "P3_22", "RdD5", "RdD4", "P3_23", "W2", "RaW5", "P3_12", "P3_13", "W1", "RaW2", "P3_01",
    "P3_02", "LdD0", "P3_03", "W0", "RaW0", "RaW1", "RaW3", "RbW5", "LbD3", "RbW2", "LdD1", "LcD2",
    "LxD3", "RbW0", "RaW4", "RbW1", "LeD0", "RbW3", "LcD3", "RcW5", "RcW2", "RdW5", "RdW2", "RcW0",
    "LeD1", "RbW4", "RdW0", "P4_00", "RcW1", "LdD2", "P4_10", "RcW3", "RdW1", "P4_01", "RcW4", "RdW3",
    "P4_02", "LdD3", "P4_11", "P4_12", "RdW4", "P4e_3", "LeD2", "P4_03", "P4_13", "E1", "P4_2", "LeD3",
    "P4_3", "E3", "E2", "E0",
)
FIRST = next(int(name[1]) for name in ORDER if name[0] == "E")


def kernel(band_in, frag_in, ham, deriv, n_out, e_out, pulay, ls, ld, rs, rq, rd, rw, mask, acc, terms, mine, by_row, by_col,
           weights, fetched, band, frag, l_send, l_recv, r_send, r_recv, t_send, t_recv, i_sem):
    r = lax.axis_index("row")
    c = lax.axis_index("col")
    z = lax.div(c, 4)
    y = lax.rem(c, 4)
    up = {"y": lax.rem(y + 1, 4), "z": lax.rem(z + 1, 4)}
    down = {"y": lax.rem(y + 3, 4), "z": lax.rem(z + 3, 4)}
    to = {
        ("y", 0): (r, z * 4 + up["y"]),
        ("y", 1): (r, z * 4 + down["y"]),
        ("z", 0): (r, up["z"] * 4 + y),
        ("z", 1): (r, down["z"] * 4 + y),
        ("x", 0): (lax.rem(r + 2, NR), c),
        ("x", 1): (lax.rem(r + 6, NR), c),
        "core": (r + 1 - 2 * lax.rem(r, 2), c),
    }
    r_up, r_down, r_far = lax.rem(r + 2, NR), lax.rem(r + 6, NR), lax.rem(r + 4, NR)

    barrier = pltpu.get_barrier_semaphore()
    for target in to.values():
        pl.semaphore_signal(barrier, inc=1, device_id=target, device_id_type=MESH)

    def drain(ref, sem):
        pltpu.make_async_copy(ref, ref, sem).wait()

    def send(ref, target, send_sem, recv_sem):
        pltpu.make_async_remote_copy(
            src_ref=ref, dst_ref=ref, send_sem=send_sem, recv_sem=recv_sem, device_id=target, device_id_type=MESH
        ).start()

    left = {"S": ls, "D": ld}
    right = {"S": rs, "Q": rq, "D": rd, "W": rw}

    def left_step(stage, x, p):
        buf, h, a = left[x], HALF[p], OFFS[p]
        out = l_send.at[p]
        both = pl.ds(a, 2 * h)
        one, two = pl.ds(a, h), pl.ds(a + h, h)
        ones = (pl.ds(a, h // 2), pl.ds(a + h // 2, h // 2))
        twos = (pl.ds(a + h, h // 2), pl.ds(a + h + h // 2, h // 2))
        backs = (down, up)
        far_y, far_z = lax.rem(y + 2, 4), lax.rem(z + 2, 4)
        if stage == "a":
            if x == "S":
                start_rows(a, 2 * h)
            for axis in "yz":
                for side in (0, 1):
                    send(buf.at[z, y, both], to[axis, side], out, l_recv.at[4 * p])
        elif stage == "b":
            drain(buf.at[0, :, both], l_recv.at[4 * p])
            for side in (0, 1):
                send(buf.at[z, backs[side]["y"], ones[side]], to["y", side], out, l_recv.at[4 * p + 1])
                send(buf.at[backs[side]["z"], y, twos[side]], to["z", side], out, l_recv.at[4 * p + 1])
        elif stage == "x":
            for back in backs:
                for side in (0, 1):
                    send(buf.at[z, back["y"], one], to["z", side], out, l_recv.at[4 * p + 2])
                    send(buf.at[back["z"], y, two], to["y", side], out, l_recv.at[4 * p + 2])
        elif stage == "c":
            drain(buf.at[0, 0, both], l_recv.at[4 * p + 1])
            for side in (0, 1):
                send(buf.at[z, far_y, one], to["z", side], out, l_recv.at[4 * p + 2])
                send(buf.at[far_z, y, two], to["y", side], out, l_recv.at[4 * p + 2])
        elif stage == "d":
            drain(buf.at[pl.ds(0, 3), :, one], l_recv.at[4 * p + 2])
            for side in (0, 1):
                send(buf.at[backs[side]["z"], :, ones[side]], to["z", side], out, l_recv.at[4 * p + 3])
                send(buf.at[:, backs[side]["y"], twos[side]], to["y", side], out, l_recv.at[4 * p + 3])
        else:
            drain(buf.at[0, :, both], l_recv.at[4 * p + 3])

    def right_step(stage, x, p):
        buf = right[x]
        a, n = PIECES[p]
        out, near, far = r_send.at[p], r_recv.at[p], r_recv.at[NS + p]
        core = r_recv.at[2 * NS + 2 * p + "SQDW".index(x) % 2]
        rows = pl.ds(a, n)
        if stage == "a":
            if x == "S":
                start_rows(a, n)
            send(buf.at[r, rows], to["x", 0], out, near)
            send(buf.at[r, rows], to["x", 1], out, near)
            send(buf.at[r, rows], to["core"], out, core)
        elif stage == "b":
            drain(buf.at[pl.ds(0, 2), rows], near)
            send(buf.at[r_down, pl.ds(a, n // 2)], to["x", 0], out, far)
            send(buf.at[r_up, pl.ds(a + n // 2, n // 2)], to["x", 1], out, far)
            send(buf.at[r_down, rows], to["core"], out, core)
            send(buf.at[r_up, rows], to["core"], out, core)
        elif stage == "c":
            drain(buf.at[0, rows], far)
            send(buf.at[r_far, rows], to["core"], out, core)
        else:
            drain(buf.at[pl.ds(0, 4), rows], core)

    def all_sent():
        for p in range(NP):
            drain(ls.at[pl.ds(0, 3), :, pl.ds(0, 5 * HALF[p])], l_send.at[p])
        for p, (_, n) in enumerate(PIECES):
            drain(ls.at[:, :, pl.ds(0, 7 * n // 4)], r_send.at[p])

    def whole(buf, panel, a, n):
        rows = pl.ds(a, n)
        acc[rows, :] = jnp.zeros((n, COLS), F32)

        def step(i, _):
            lhs = jnp.concatenate([buf[i, j, rows, :] for j in range(4)], axis=1)
            rhs = panel[pl.ds(2 * i, 2)].reshape(4 * COLS, COLS)
            acc[rows, :] += jnp.dot(lhs, rhs, preferred_element_type=F32)
            return 0

        lax.fori_loop(0, 4, step, 0)

    def part(buf, panel, a, n, q):
        rows = pl.ds(a, n)
        lo, size = PART[q]
        group = 1024 // size

        def piece(i, j):
            zz = i * (group // 2) + j // 2
            cols = []
            for half in (0, 1):
                s, e = max(lo, half * COLS), min(lo + size, (half + 1) * COLS)
                if s < e:
                    cols.append(buf[zz, 2 * (j % 2) + half, rows, s - half * COLS : e - half * COLS])
            return cols

        def step(i, _):
            lhs = jnp.concatenate([v for j in range(group) for v in piece(i, j)], axis=1)
            rhs = panel[pl.ds(group * i, group), pl.ds(lo, size), :].reshape(1024, COLS)
            acc[rows, :] += jnp.dot(lhs, rhs, preferred_element_type=F32)
            return 0

        if q == 0:
            acc[rows, :] = jnp.zeros((n, COLS), F32)
        if NR == group:
            step(0, 0)
        else:
            lax.fori_loop(0, NR // group, step, 0)

    def fetch(i):
        if i < 3:
            rows = pl.ds(256 * i, 256)
            return pltpu.make_async_copy(ham.at[rows], fetched.at[0, rows], i_sem.at[i])
        src, dst = ((deriv, fetched.at[1]), (band_in, band), (frag_in, frag))[i - 3]
        return pltpu.make_async_copy(src, dst, i_sem.at[i])

    def split(buf, panel, early):
        h = HALF[LAST]
        one, two, both = pl.ds(OFFS[LAST], h), pl.ds(OFFS[LAST] + h, h), pl.ds(OFFS[LAST], 2 * h)
        zs, ys = (lax.rem(z + 2, 4), z, up["z"], down["z"]), (lax.rem(y + 2, 4), y, up["y"], down["y"])

        def add(rows, blocks):
            lhs = jnp.concatenate([buf[zz, yy, rows, :] for zz, yy in blocks], axis=1)
            half = [pl.ds(pl.multiple_of(lax.rem(yy, 2) * COLS, COLS), COLS) for _, yy in blocks]
            rhs = jnp.concatenate(
                [panel[2 * zz + lax.div(yy, 2), part_of, :] for (zz, yy), part_of in zip(blocks, half)], axis=0
            )
            acc[rows, :] += jnp.dot(lhs, rhs, preferred_element_type=F32)

        if early:
            acc[both, :] = jnp.zeros((2 * h, COLS), F32)

            def step(i, _):
                zz = lax.rem(z + i + lax.div(i, 2), 4)
                add(both, [(zz, yy) for yy in ys[1:]])
                return 0

            lax.fori_loop(0, 3, step, 0)
            add(one, [(zz, ys[0]) for zz in zs[1:]])
            add(two, [(zs[0], yy) for yy in ys[1:]])
        else:
            add(one, [(zs[0], yy) for yy in ys])
            add(two, [(zz, ys[0]) for zz in zs])

    first = int(ORDER[0][3])
    first = (OFFS if ORDER[0][0] == "L" else [a for a, _ in PIECES])[first] // 256
    order_of_rows = (first, *(i for i in range(3) if i != first))
    ready = {}

    def start_rows(a, n):
        for i in range(a // BLK, (a + n + BLK - 1) // BLK):
            if i in ready:
                continue
            if not ready:
                fetch(4).wait()
            if i // 2 not in ready.values():
                fetch(i // 2).wait()
            ready[i] = i // 2
            rows = pl.ds(i * BLK, BLK)
            for j in range(3):
                row, col, cols = r * 6 + i, c * 3 + j, pl.ds(j * BLK, BLK)
                inside = jnp.abs(row - col) <= jnp.maximum(band[row], band[col])
                block = jnp.full((BLK, BLK), jnp.where(inside, 1.0, 0.0), F32)
                mask[rows, cols] = block
                start = (fetched[0, rows, cols].astype(F32) * block).astype(BF16)
                rs[r, rows, cols] = start
                ls[z, y, rows, cols] = start

    def begin():
        for i in (4, *order_of_rows, 5, 3):
            fetch(i).start()
        terms[...] = jnp.zeros((8, COLS), F32)
        start_rows(256 * order_of_rows[0], 256)
        pl.semaphore_wait(barrier, len(to))

    def prepare():
        fetch(5).wait()
        for f in (0, 1):
            for j in range(3 * NC):
                weight = jnp.where(frag[j] == 2 * c + f, 1.0, 0.0)
                weights[f, j // 3, :, pl.ds(j % 3 * BLK, BLK)] = jnp.full((1, BLK), weight, F32)

    def square_rows(p):
        a, n = OFFS[p], 2 * HALF[p]
        if p == LAST:
            split(ls, rs, False)
        else:
            whole(ls, rs, a, n)
        rq[r, pl.ds(a, n), :] = (acc[pl.ds(a, n), :] * mask[pl.ds(a, n), :]).astype(BF16)

    def density_rows(p):
        a, n = OFFS[p], 2 * HALF[p]
        rows = pl.ds(a, n)
        sign = 1.5 * rs[r, rows, :].astype(F32) - 0.5 * acc[rows, :]
        sign = (mask[rows, :] * sign).astype(BF16)
        n_out[rows, :] = sign
        line = r * ROWS + a + lax.broadcasted_iota(jnp.int32, (n, COLS), 0)
        column = c * COLS + lax.broadcasted_iota(jnp.int32, (n, COLS), 1)
        identity = jnp.where(line == column, 1.0, 0.0)
        density = (0.5 * (identity - sign.astype(F32))).astype(BF16)
        rd[r, rows, :] = density
        ld[z, y, rows, :] = density

    def weighted_rows(u):
        rows = pl.ds(256 * u, 256)
        rw[r, rows, :] = (acc[rows, :] * mask[rows, :]).astype(BF16)

    def energy_rows(p):
        a, n = OFFS[p], 2 * HALF[p]
        rows = pl.ds(a, n)
        if p == FIRST:
            fetch(3).wait()
        energy = (acc[rows, :] * mask[rows, :]).astype(BF16)
        e_out[rows, :] = energy
        product = energy.astype(F32) * fetched[1, rows, :].astype(F32)
        terms[...] += jnp.sum(product.reshape(n // 8, 8, COLS), axis=0)

    def finish():
        mine[...] = jnp.sum(terms[...], axis=0, keepdims=True)
        by_row[r] = mine[...]
        for k in (4, 2, 6, 0):
            for other in (True, False):
                if k == 0 and not other:
                    continue
                peer = lax.rem(r + k, NR)
                peer = peer + 1 - 2 * lax.rem(r, 2) if other else peer
                pltpu.make_async_remote_copy(
                    src_ref=mine, dst_ref=by_row.at[r], send_sem=t_send.at[0], recv_sem=t_recv.at[0],
                    device_id=(peer, c), device_id_type=MESH,
                ).start()
        drain(by_row.at[pl.ds(0, NR - 1)], t_recv.at[0])
        by_col[c] = jnp.sum(by_row[...], axis=0)
        steps = sorted(range(1, NC), key=lambda k: -min(k // 4, 4 - k // 4) - min(k % 4, 4 - k % 4))
        for k in steps:
            peer = lax.rem(z + k // 4, 4) * 4 + lax.rem(y + k % 4, 4)
            send(by_col.at[c], (r, peer), t_send.at[1], t_recv.at[1])
        all_sent()
        drain(by_row.at[pl.ds(0, NR - 1)], t_send.at[0])
        drain(by_col.at[pl.ds(0, NC - 1)], t_recv.at[1])
        for f in (0, 1):
            picked = jnp.sum(weights[f] * by_col[...], axis=0)
            pulay[pl.ds(f, 1), :] = picked[:, :BLK] + picked[:, BLK : 2 * BLK] + picked[:, 2 * BLK :]
        drain(by_col.at[pl.ds(0, NC - 1)], t_send.at[1])

    begin()
    for name in ORDER:
        digits = [int(d) for d in name if d.isdigit()]
        if name[0] == "L":
            left_step(name[1], name[2], digits[0])
        elif name[0] == "R":
            right_step(name[1], name[2], digits[0])
        elif name[:3] in ("P1e", "P4e"):
            split(*((ls, rs) if name[1] == "1" else (ld, rw)), True)
        elif name[:2] == "P1":
            square_rows(digits[1])
        elif name[:2] in ("P2", "P3"):
            part(ls, rq if name[1] == "2" else rd, 256 * digits[1], 256, digits[2])
        elif name[:2] == "P4":
            p = digits[1]
            if len(digits) == 3:
                part(ld, rw, OFFS[p], 2 * HALF[p], digits[2])
            elif p == LAST:
                split(ld, rw, False)
            else:
                whole(ld, rw, OFFS[p], 2 * HALF[p])
        elif name[0] == "N":
            density_rows(digits[0])
        elif name[0] == "W":
            weighted_rows(digits[0])
        elif name[0] == "E":
            energy_rows(digits[0])
        else:
            prepare()
    finish()


def write_out(n_in, e_in, p_in, n_out, e_out, p_out, sems):
    copies = [
        pltpu.make_async_copy(src, dst, sems.at[i])
        for i, (src, dst) in enumerate(((n_in, n_out), (e_in, e_out), (p_in, p_out)))
    ]
    for copy in copies:
        copy.start()
    for copy in copies:
        copy.wait()


def step(ham, deriv, band, frag_of):
    vmem = pl.BlockSpec(memory_space=pltpu.VMEM)
    hbm = pl.BlockSpec(memory_space=pl.ANY)
    dma = pltpu.SemaphoreType.DMA
    panel = pltpu.VMEM((NR, ROWS, COLS), BF16)
    slab = pltpu.VMEM((4, 4, ROWS, COLS), BF16)
    shapes = (((ROWS, COLS), BF16), ((ROWS, COLS), BF16), ((2, BLK), F32))
    held = pl.pallas_call(
        kernel,
        out_shape=tuple(pltpu.VMEM(*shape) for shape in shapes),
        in_specs=[hbm, hbm, hbm, hbm],
        out_specs=(vmem, vmem, vmem),
        scratch_shapes=[
            slab, slab, panel, panel, panel, panel,
            pltpu.VMEM((ROWS, COLS), F32),
            pltpu.VMEM((ROWS, COLS), F32),
            pltpu.VMEM((8, COLS), F32),
            pltpu.VMEM((1, COLS), F32),
            pltpu.VMEM((NR, 1, COLS), F32),
            pltpu.VMEM((NC, 1, COLS), F32),
            pltpu.VMEM((2, NC, 1, COLS), F32),
            pltpu.VMEM((2, ROWS, COLS), BF16),
            pltpu.SMEM((6 * NR,), jnp.int32),
            pltpu.SMEM((6 * NR,), jnp.int32),
            dma((NP,)), dma((4 * NP,)), dma((NS,)), dma((4 * NS,)), dma((2,)), dma((2,)), dma((6,)),
        ],
        compiler_params=pltpu.CompilerParams(collective_id=0, has_side_effects=True, vmem_limit_bytes=56 << 20),
        name="sign_step",
    )(band, frag_of, ham, deriv)
    return pl.pallas_call(
        write_out,
        out_shape=tuple(jax.ShapeDtypeStruct(*shape) for shape in shapes),
        in_specs=[vmem, vmem, vmem],
        out_specs=(hbm, hbm, hbm),
        scratch_shapes=[dma((3,))],
        name="write_out",
    )(*(pltpu.with_memory_space_constraint(x, pltpu.VMEM) for x in held))


def solution(mesh):
    return jax.shard_map(
        step,
        mesh=mesh,
        in_specs=(P("row", "col"), P("row", "col"), P(), P()),
        out_specs=(P("row", "col"), P("row", "col"), P("col", None)),
        check_vma=False,
    )
```

```python
import functools

import jax
import jax.numpy as jnp
from jax import lax
from jax.experimental import pallas as pl
from jax.experimental.pallas import tpu as pltpu
from jax.sharding import PartitionSpec as P

MESH = pl.DeviceIdType.MESH
BLK = 128
ROWS = 768
COLS = 384
NR = 8
NC = 16
F32 = jnp.float32
BF16 = jnp.bfloat16
OFFS = (0, 256, 512, 640)
HALF = (128, 128, 64, 64)
NP = len(HALF)
PIECES = ((0, 256), (256, 128), (384, 128), (512, 128), (640, 64), (704, 64))
NS = len(PIECES)
LAST = NP - 1
PART = ((0, 256), (256, 256), (512, 128), (640, 128))
ORDER = (
    "LaS3", "RaS1", "LaS0", "prep", "RaS3", "LaS1", "RaS0", "RaS2", "RbS1", "RbS3", "LbS0", "LxS0",
    "RbS0", "LbS1", "RbS2", "RaS5", "LcS0", "LxS1", "RcS1", "LaS2", "RcS3", "RaS4", "RdS1", "RdS3",
    "RcS0", "RcS2", "RdS0", "LcS1", "RbS5", "RdS2", "RbS4", "LdS0", "RcS5", "RcS4", "RdS5", "RdS4",
    "LbS2", "LdS1", "LxS2", "LbS3", "LeS0", "P1_0", "RaQ0", "LcS2", "LxS3", "LeS1", "P1_1", "RaQ1",
    "RaQ2", "LcS3", "LdS2", "RbQ0", "RbQ1", "LdS3", "P1e_3", "RbQ2", "LeS2", "P1_2", "RaQ3", "RcQ0",
    "LeS3", "P1_3", "RaQ5", "RaQ4", "RcQ1", "RdQ0", "P2_10", "P2_20", "RdQ1", "RcQ2", "P2_00", "RbQ3",
    "RdQ2", "P2_01", "RbQ5", "P2_11", "RbQ4", "P2_21", "RcQ3", "RcQ5", "RdQ3", "P2_12", "RcQ4", "P2_02",
    "RdQ5", "P2_22", "RdQ4", "P2_03", "N0", "RaD0", "LaD0", "P2_13", "N1", "RaD1", "LaD1", "RaD2",
    "P2_23", "N2", "LaD2", "RaD3", "N3", "RaD5", "RbD0", "RaD4", "LbD0", "LxD0", "RbD1", "RbD2",
    "LbD1", "LxD1", "RbD3", "RbD5", "LcD0", "LaD3", "RcD0", "RbD4", "RdD0", "P3_10", "RcD1", "P3_20",
    "LcD1", "LbD2", "LxD2", "RcD2", "P3_00", "RdD1", "RcD3", "RdD2", "P3_11", "RcD4", "RcD5", "P3_21",
    "RdD3", "P3_22", "RdD5", "RdD4", "P3_23", "W2", "RaW5", "P3_12", "P3_13", "W1", "RaW2", "P3_01",
    "P3_02", "LdD0", "P3_03", "W0", "RaW0", "RaW1", "RaW3", "RbW5", "LbD3", "RbW2", "LdD1", "LcD2",
    "LxD3", "RbW0", "RaW4", "RbW1", "LeD0", "RbW3", "LcD3", "RcW5", "RcW2", "RdW5", "RdW2", "RcW0",
    "LeD1", "RbW4", "RdW0", "P4_00", "RcW1", "LdD2", "P4_10", "RcW3", "RdW1", "P4_01", "RcW4", "RdW3",
    "P4_02", "LdD3", "P4_11", "P4_12", "RdW4", "P4e_3", "LeD2", "P4_03", "P4_13", "E1", "E0", "P4_2", "E2",
    "LeD3", "P4_3", "E3",
)
FIRST = next(int(name[1]) for name in ORDER if name[0] == "E")


def kernel(band_in, frag_in, ham, deriv, n_out, e_out, pulay, ls, ld, rs, rq, rd, rw, mask, acc, terms, mine, by_row, by_col,
           weights, fetched, band, frag, l_send, l_recv, r_send, r_recv, t_send, t_recv, i_sem):
    r = lax.axis_index("row")
    c = lax.axis_index("col")
    z = lax.div(c, 4)
    y = lax.rem(c, 4)
    up = {"y": lax.rem(y + 1, 4), "z": lax.rem(z + 1, 4)}
    down = {"y": lax.rem(y + 3, 4), "z": lax.rem(z + 3, 4)}
    to = {
        ("y", 0): (r, z * 4 + up["y"]),
        ("y", 1): (r, z * 4 + down["y"]),
        ("z", 0): (r, up["z"] * 4 + y),
        ("z", 1): (r, down["z"] * 4 + y),
        ("x", 0): (lax.rem(r + 2, NR), c),
        ("x", 1): (lax.rem(r + 6, NR), c),
        "core": (r + 1 - 2 * lax.rem(r, 2), c),
    }
    r_up, r_down, r_far = lax.rem(r + 2, NR), lax.rem(r + 6, NR), lax.rem(r + 4, NR)

    barrier = pltpu.get_barrier_semaphore()
    for target in to.values():
        pl.semaphore_signal(barrier, inc=1, device_id=target, device_id_type=MESH)

    def drain(ref, sem):
        pltpu.make_async_copy(ref, ref, sem).wait()

    def send(ref, target, send_sem, recv_sem):
        pltpu.make_async_remote_copy(
            src_ref=ref, dst_ref=ref, send_sem=send_sem, recv_sem=recv_sem, device_id=target, device_id_type=MESH
        ).start()

    left = {"S": ls, "D": ld}
    right = {"S": rs, "Q": rq, "D": rd, "W": rw}

    def left_step(stage, x, p):
        buf, h, a = left[x], HALF[p], OFFS[p]
        out = l_send.at[p]
        both = pl.ds(a, 2 * h)
        one, two = pl.ds(a, h), pl.ds(a + h, h)
        ones = (pl.ds(a, h // 2), pl.ds(a + h // 2, h // 2))
        twos = (pl.ds(a + h, h // 2), pl.ds(a + h + h // 2, h // 2))
        backs = (down, up)
        far_y, far_z = lax.rem(y + 2, 4), lax.rem(z + 2, 4)
        if stage == "a":
            if x == "S":
                start_rows(a, 2 * h)
            for axis in "yz":
                for side in (0, 1):
                    send(buf.at[z, y, both], to[axis, side], out, l_recv.at[4 * p])
        elif stage == "b":
            drain(buf.at[0, :, both], l_recv.at[4 * p])
            for side in (0, 1):
                send(buf.at[z, backs[side]["y"], ones[side]], to["y", side], out, l_recv.at[4 * p + 1])
                send(buf.at[backs[side]["z"], y, twos[side]], to["z", side], out, l_recv.at[4 * p + 1])
        elif stage == "x":
            for back in backs:
                for side in (0, 1):
                    send(buf.at[z, back["y"], one], to["z", side], out, l_recv.at[4 * p + 2])
                    send(buf.at[back["z"], y, two], to["y", side], out, l_recv.at[4 * p + 2])
        elif stage == "c":
            drain(buf.at[0, 0, both], l_recv.at[4 * p + 1])
            for side in (0, 1):
                send(buf.at[z, far_y, one], to["z", side], out, l_recv.at[4 * p + 2])
                send(buf.at[far_z, y, two], to["y", side], out, l_recv.at[4 * p + 2])
        elif stage == "d":
            drain(buf.at[pl.ds(0, 3), :, one], l_recv.at[4 * p + 2])
            for side in (0, 1):
                send(buf.at[backs[side]["z"], :, ones[side]], to["z", side], out, l_recv.at[4 * p + 3])
                send(buf.at[:, backs[side]["y"], twos[side]], to["y", side], out, l_recv.at[4 * p + 3])
        else:
            drain(buf.at[0, :, both], l_recv.at[4 * p + 3])

    def right_step(stage, x, p):
        buf = right[x]
        a, n = PIECES[p]
        out, near, far = r_send.at[p], r_recv.at[p], r_recv.at[NS + p]
        core = r_recv.at[2 * NS + 2 * p + "SQDW".index(x) % 2]
        rows = pl.ds(a, n)
        if stage == "a":
            if x == "S":
                start_rows(a, n)
            send(buf.at[r, rows], to["x", 0], out, near)
            send(buf.at[r, rows], to["x", 1], out, near)
            send(buf.at[r, rows], to["core"], out, core)
        elif stage == "b":
            drain(buf.at[pl.ds(0, 2), rows], near)
            send(buf.at[r_down, pl.ds(a, n // 2)], to["x", 0], out, far)
            send(buf.at[r_up, pl.ds(a + n // 2, n // 2)], to["x", 1], out, far)
            send(buf.at[r_down, rows], to["core"], out, core)
            send(buf.at[r_up, rows], to["core"], out, core)
        elif stage == "c":
            drain(buf.at[0, rows], far)
            send(buf.at[r_far, rows], to["core"], out, core)
        else:
            drain(buf.at[pl.ds(0, 4), rows], core)

    def all_sent():
        for p in range(NP):
            drain(ls.at[pl.ds(0, 3), :, pl.ds(0, 5 * HALF[p])], l_send.at[p])
        for p, (_, n) in enumerate(PIECES):
            drain(ls.at[:, :, pl.ds(0, 7 * n // 4)], r_send.at[p])

    def whole(buf, panel, a, n):
        rows = pl.ds(a, n)
        acc[rows, :] = jnp.zeros((n, COLS), F32)

        def step(i, _):
            lhs = jnp.concatenate([buf[i, j, rows, :] for j in range(4)], axis=1)
            rhs = panel[pl.ds(2 * i, 2)].reshape(4 * COLS, COLS)
            acc[rows, :] += jnp.dot(lhs, rhs, preferred_element_type=F32)
            return 0

        lax.fori_loop(0, 4, step, 0)

    def part(buf, panel, a, n, q):
        rows = pl.ds(a, n)
        lo, size = PART[q]
        group = 1024 // size

        def piece(i, j):
            zz = i * (group // 2) + j // 2
            cols = []
            for half in (0, 1):
                s, e = max(lo, half * COLS), min(lo + size, (half + 1) * COLS)
                if s < e:
                    cols.append(buf[zz, 2 * (j % 2) + half, rows, s - half * COLS : e - half * COLS])
            return cols

        def step(i, _):
            lhs = jnp.concatenate([v for j in range(group) for v in piece(i, j)], axis=1)
            rhs = panel[pl.ds(group * i, group), pl.ds(lo, size), :].reshape(1024, COLS)
            acc[rows, :] += jnp.dot(lhs, rhs, preferred_element_type=F32)
            return 0

        if q == 0:
            acc[rows, :] = jnp.zeros((n, COLS), F32)
        if NR == group:
            step(0, 0)
        else:
            lax.fori_loop(0, NR // group, step, 0)

    def fetch(i):
        if i < 3:
            rows = pl.ds(256 * i, 256)
            return pltpu.make_async_copy(ham.at[rows], fetched.at[0, rows], i_sem.at[i])
        src, dst = ((deriv, fetched.at[1]), (band_in, band), (frag_in, frag))[i - 3]
        return pltpu.make_async_copy(src, dst, i_sem.at[i])

    def split(buf, panel, early):
        h = HALF[LAST]
        one, two, both = pl.ds(OFFS[LAST], h), pl.ds(OFFS[LAST] + h, h), pl.ds(OFFS[LAST], 2 * h)
        zs, ys = (lax.rem(z + 2, 4), z, up["z"], down["z"]), (lax.rem(y + 2, 4), y, up["y"], down["y"])

        def add(rows, blocks):
            lhs = jnp.concatenate([buf[zz, yy, rows, :] for zz, yy in blocks], axis=1)
            half = [pl.ds(pl.multiple_of(lax.rem(yy, 2) * COLS, COLS), COLS) for _, yy in blocks]
            rhs = jnp.concatenate(
                [panel[2 * zz + lax.div(yy, 2), part_of, :] for (zz, yy), part_of in zip(blocks, half)], axis=0
            )
            acc[rows, :] += jnp.dot(lhs, rhs, preferred_element_type=F32)

        if early:
            acc[both, :] = jnp.zeros((2 * h, COLS), F32)

            def step(i, _):
                zz = lax.rem(z + i + lax.div(i, 2), 4)
                add(both, [(zz, yy) for yy in ys[1:]])
                return 0

            lax.fori_loop(0, 3, step, 0)
            add(one, [(zz, ys[0]) for zz in zs[1:]])
            add(two, [(zs[0], yy) for yy in ys[1:]])
        else:
            add(one, [(zs[0], yy) for yy in ys])
            add(two, [(zz, ys[0]) for zz in zs])

    first = int(ORDER[0][3])
    first = (OFFS if ORDER[0][0] == "L" else [a for a, _ in PIECES])[first] // 256
    order_of_rows = (first, *(i for i in range(3) if i != first))
    ready = {}

    def start_rows(a, n):
        for i in range(a // BLK, (a + n + BLK - 1) // BLK):
            if i in ready:
                continue
            if not ready:
                fetch(4).wait()
            if i // 2 not in ready.values():
                fetch(i // 2).wait()
            ready[i] = i // 2
            rows = pl.ds(i * BLK, BLK)
            for j in range(3):
                row, col, cols = r * 6 + i, c * 3 + j, pl.ds(j * BLK, BLK)
                inside = jnp.abs(row - col) <= jnp.maximum(band[row], band[col])
                block = jnp.full((BLK, BLK), jnp.where(inside, 1.0, 0.0), F32)
                mask[rows, cols] = block
                start = (fetched[0, rows, cols].astype(F32) * block).astype(BF16)
                rs[r, rows, cols] = start
                ls[z, y, rows, cols] = start

    def begin():
        for i in (4, *order_of_rows, 5, 3):
            fetch(i).start()
        terms[...] = jnp.zeros((8, COLS), F32)
        start_rows(256 * order_of_rows[0], 256)
        pl.semaphore_wait(barrier, len(to))

    def prepare():
        fetch(5).wait()
        for f in (0, 1):
            for j in range(3 * NC):
                weight = jnp.where(frag[j] == 2 * c + f, 1.0, 0.0)
                weights[f, j // 3, :, pl.ds(j % 3 * BLK, BLK)] = jnp.full((1, BLK), weight, F32)

    def square_rows(p):
        a, n = OFFS[p], 2 * HALF[p]
        if p == LAST:
            split(ls, rs, False)
        else:
            whole(ls, rs, a, n)
        rq[r, pl.ds(a, n), :] = (acc[pl.ds(a, n), :] * mask[pl.ds(a, n), :]).astype(BF16)

    def density_rows(p):
        a, n = OFFS[p], 2 * HALF[p]
        rows = pl.ds(a, n)
        sign = 1.5 * rs[r, rows, :].astype(F32) - 0.5 * acc[rows, :]
        sign = (mask[rows, :] * sign).astype(BF16)
        n_out[rows, :] = sign
        line = r * ROWS + a + lax.broadcasted_iota(jnp.int32, (n, COLS), 0)
        column = c * COLS + lax.broadcasted_iota(jnp.int32, (n, COLS), 1)
        identity = jnp.where(line == column, 1.0, 0.0)
        density = (0.5 * (identity - sign.astype(F32))).astype(BF16)
        rd[r, rows, :] = density
        ld[z, y, rows, :] = density

    def weighted_rows(u):
        rows = pl.ds(256 * u, 256)
        rw[r, rows, :] = (acc[rows, :] * mask[rows, :]).astype(BF16)

    def energy_rows(p):
        a, n = OFFS[p], 2 * HALF[p]
        rows = pl.ds(a, n)
        if p == FIRST:
            fetch(3).wait()
        energy = (acc[rows, :] * mask[rows, :]).astype(BF16)
        e_out[rows, :] = energy
        product = energy.astype(F32) * fetched[1, rows, :].astype(F32)
        terms[...] += jnp.sum(product.reshape(n // 8, 8, COLS), axis=0)

    def finish():
        mine[...] = jnp.sum(terms[...], axis=0, keepdims=True)
        by_row[r] = mine[...]
        for k in (4, 2, 6, 0):
            for other in (True, False):
                if k == 0 and not other:
                    continue
                peer = lax.rem(r + k, NR)
                peer = peer + 1 - 2 * lax.rem(r, 2) if other else peer
                pltpu.make_async_remote_copy(
                    src_ref=mine, dst_ref=by_row.at[r], send_sem=t_send.at[0], recv_sem=t_recv.at[0],
                    device_id=(peer, c), device_id_type=MESH,
                ).start()
        drain(by_row.at[pl.ds(0, NR - 1)], t_recv.at[0])
        by_col[c] = jnp.sum(by_row[...], axis=0)
        steps = sorted(range(1, NC), key=lambda k: -min(k // 4, 4 - k // 4) - min(k % 4, 4 - k % 4))
        for k in steps:
            peer = lax.rem(z + k // 4, 4) * 4 + lax.rem(y + k % 4, 4)
            send(by_col.at[c], (r, peer), t_send.at[1], t_recv.at[1])
        all_sent()
        drain(by_row.at[pl.ds(0, NR - 1)], t_send.at[0])
        drain(by_col.at[pl.ds(0, NC - 1)], t_recv.at[1])
        for f in (0, 1):
            picked = jnp.sum(weights[f] * by_col[...], axis=0)
            pulay[pl.ds(f, 1), :] = picked[:, :BLK] + picked[:, BLK : 2 * BLK] + picked[:, 2 * BLK :]
        drain(by_col.at[pl.ds(0, NC - 1)], t_send.at[1])

    begin()
    for name in ORDER:
        digits = [int(d) for d in name if d.isdigit()]
        if name[0] == "L":
            left_step(name[1], name[2], digits[0])
        elif name[0] == "R":
            right_step(name[1], name[2], digits[0])
        elif name[:3] in ("P1e", "P4e"):
            split(*((ls, rs) if name[1] == "1" else (ld, rw)), True)
        elif name[:2] == "P1":
            square_rows(digits[1])
        elif name[:2] in ("P2", "P3"):
            part(ls, rq if name[1] == "2" else rd, 256 * digits[1], 256, digits[2])
        elif name[:2] == "P4":
            p = digits[1]
            if len(digits) == 3:
                part(ld, rw, OFFS[p], 2 * HALF[p], digits[2])
            elif p == LAST:
                split(ld, rw, False)
            else:
                whole(ld, rw, OFFS[p], 2 * HALF[p])
        elif name[0] == "N":
            density_rows(digits[0])
        elif name[0] == "W":
            weighted_rows(digits[0])
        elif name[0] == "E":
            energy_rows(digits[0])
        else:
            prepare()
    finish()


def write_out(n_in, e_in, p_in, n_out, e_out, p_out, sems):
    pairs = [
        (src.at[pl.ds(192 * i, 192)], dst.at[pl.ds(192 * i, 192)])
        for src, dst in ((n_in, n_out), (e_in, e_out))
        for i in range(ROWS // 192)
    ]
    pairs.append((p_in, p_out))
    copies = [pltpu.make_async_copy(src, dst, sems.at[i]) for i, (src, dst) in enumerate(pairs)]
    for copy in copies:
        copy.start()
    for copy in copies:
        copy.wait()


def step(ham, deriv, band, frag_of):
    vmem = pl.BlockSpec(memory_space=pltpu.VMEM)
    hbm = pl.BlockSpec(memory_space=pl.ANY)
    dma = pltpu.SemaphoreType.DMA
    panel = pltpu.VMEM((NR, ROWS, COLS), BF16)
    slab = pltpu.VMEM((4, 4, ROWS, COLS), BF16)
    shapes = (((ROWS, COLS), BF16), ((ROWS, COLS), BF16), ((2, BLK), F32))
    held = pl.pallas_call(
        kernel,
        out_shape=tuple(pltpu.VMEM(*shape) for shape in shapes),
        in_specs=[hbm, hbm, hbm, hbm],
        out_specs=(vmem, vmem, vmem),
        scratch_shapes=[
            slab, slab, panel, panel, panel, panel,
            pltpu.VMEM((ROWS, COLS), F32),
            pltpu.VMEM((ROWS, COLS), F32),
            pltpu.VMEM((8, COLS), F32),
            pltpu.VMEM((1, COLS), F32),
            pltpu.VMEM((NR, 1, COLS), F32),
            pltpu.VMEM((NC, 1, COLS), F32),
            pltpu.VMEM((2, NC, 1, COLS), F32),
            pltpu.VMEM((2, ROWS, COLS), BF16),
            pltpu.SMEM((6 * NR,), jnp.int32),
            pltpu.SMEM((6 * NR,), jnp.int32),
            dma((NP,)), dma((4 * NP,)), dma((NS,)), dma((4 * NS,)), dma((2,)), dma((2,)), dma((6,)),
        ],
        compiler_params=pltpu.CompilerParams(collective_id=0, has_side_effects=True, vmem_limit_bytes=56 << 20),
        name="sign_step",
    )(band, frag_of, ham, deriv)
    return pl.pallas_call(
        write_out,
        out_shape=tuple(jax.ShapeDtypeStruct(*shape) for shape in shapes),
        in_specs=[vmem, vmem, vmem],
        out_specs=(hbm, hbm, hbm),
        scratch_shapes=[dma((9,))],
        name="write_out",
    )(*(pltpu.with_memory_space_constraint(x, pltpu.VMEM) for x in held))


def solution(mesh):
    return jax.shard_map(
        step,
        mesh=mesh,
        in_specs=(P("row", "col"), P("row", "col"), P(), P()),
        out_specs=(P("row", "col"), P("row", "col"), P("col", None)),
        check_vma=False,
    )
```

```python
import functools

import jax
import jax.numpy as jnp
from jax import lax
from jax.experimental import pallas as pl
from jax.experimental.pallas import tpu as pltpu
from jax.sharding import PartitionSpec as P

MESH = pl.DeviceIdType.MESH
BLK = 128
ROWS = 768
COLS = 384
NR = 8
NC = 16
F32 = jnp.float32
BF16 = jnp.bfloat16
OFFS = (0, 256, 512, 640)
HALF = (128, 128, 64, 64)
NP = len(HALF)
PIECES = ((0, 256), (256, 128), (384, 128), (512, 128), (640, 64), (704, 64))
NS = len(PIECES)
LAST = NP - 1
PART = ((0, 256), (256, 256), (512, 128), (640, 128))
ORDER = (
    "RaS0", "LaS1", "LaS0", "prep", "RbS0", "RaS4", "RaS3", "RaS5", "LbS1", "LxS1", "RcS0", "RaS1",
    "RaS2", "LbS0", "LxS0", "RbS4", "LcS1", "RdS0", "RbS3", "RbS5", "RbS1", "LcS0", "LaS2", "RbS2",
    "RcS4", "RcS3", "RdS4", "RcS5", "RdS3", "RcS1", "RdS5", "RcS2", "RdS1", "LdS1", "RdS2", "LdS0",
    "LaS3", "LbS2", "LxS2", "LeS1", "P1_1", "RaQ2", "LeS0", "P1_0", "LbS3", "RaQ0", "RaQ1", "RbQ2",
    "LcS2", "LxS3", "LcS3", "LdS2", "RbQ0", "LdS3", "P1e_3", "RbQ1", "LeS2", "P1_2", "RcQ2", "RaQ3",
    "LeS3", "P1_3", "RcQ0", "RdQ2", "RaQ5", "RcQ1", "RaQ4", "RdQ0", "P2_20", "RdQ1", "P2_10", "RbQ3",
    "P2_11", "RbQ5", "P2_00", "RbQ4", "P2_01", "P2_21", "RcQ3", "RcQ5", "RcQ4", "RdQ3", "P2_02", "P2_12",
    "RdQ5", "RdQ4", "P2_03", "N0", "RaD0", "LaD0", "P2_13", "N1", "RaD2", "P2_22", "P2_23", "N3",
    "LaD3", "N2", "LaD2", "RaD3", "RbD0", "RaD1", "LbD0", "LxD0", "LaD1", "RaD4", "RaD5", "RbD2",
    "RbD3", "LbD2", "LxD2", "LcD0", "RcD0", "RdD0", "P3_00", "RbD1", "P3_10", "RbD4", "P3_20", "RbD5",
    "RcD2", "RcD3", "RdD2", "RcD1", "LbD1", "LxD1", "RdD3", "RcD4", "LcD2", "RcD5", "RdD1", "P3_01",
    "P3_02", "RdD4", "RdD5", "P3_03", "W0", "RaW0", "P3_21", "P3_22", "P3_11", "LdD0", "LbD3", "P3_12",
    "P3_13", "LcD1", "LxD3", "W1", "RaW1", "RaW2", "P3_23", "W2", "RaW3", "RaW4", "RbW0", "LdD2",
    "RbW1", "RaW5", "RbW2", "LeD0", "RbW3", "LcD3", "RbW4", "LdD1", "RcW0", "RcW1", "RdW0", "P4_00",
    "RdW1", "RbW5", "RcW2", "LeD2", "P4_20", "RcW3", "RdW2", "P4_21", "LdD3", "RcW4", "P4_01", "RcW5",
    "RdW3", "P4_02", "RdW4", "P4_22", "RdW5", "P4_23", "E2", "P4_03", "E0", "P4e_3", "LeD1", "P4_10",
    "P4_11", "LeD3", "P4_3", "E3", "P4_12", "P4_13", "E1",
)
FIRST = next(int(name[1]) for name in ORDER if name[0] == "E")


def kernel(band_in, frag_in, ham, deriv, n_out, e_out, pulay, ls, ld, rs, rq, rd, rw, mask, acc, terms, mine, by_row, by_col,
           weights, fetched, band, frag, l_send, l_recv, r_send, r_recv, t_send, t_recv, i_sem):
    r = lax.axis_index("row")
    c = lax.axis_index("col")
    z = lax.div(c, 4)
    y = lax.rem(c, 4)
    up = {"y": lax.rem(y + 1, 4), "z": lax.rem(z + 1, 4)}
    down = {"y": lax.rem(y + 3, 4), "z": lax.rem(z + 3, 4)}
    to = {
        ("y", 0): (r, z * 4 + up["y"]),
        ("y", 1): (r, z * 4 + down["y"]),
        ("z", 0): (r, up["z"] * 4 + y),
        ("z", 1): (r, down["z"] * 4 + y),
        ("x", 0): (lax.rem(r + 2, NR), c),
        ("x", 1): (lax.rem(r + 6, NR), c),
        "core": (r + 1 - 2 * lax.rem(r, 2), c),
    }
    r_up, r_down, r_far = lax.rem(r + 2, NR), lax.rem(r + 6, NR), lax.rem(r + 4, NR)

    barrier = pltpu.get_barrier_semaphore()
    for target in to.values():
        pl.semaphore_signal(barrier, inc=1, device_id=target, device_id_type=MESH)

    def drain(ref, sem):
        pltpu.make_async_copy(ref, ref, sem).wait()

    def send(ref, target, send_sem, recv_sem):
        pltpu.make_async_remote_copy(
            src_ref=ref, dst_ref=ref, send_sem=send_sem, recv_sem=recv_sem, device_id=target, device_id_type=MESH
        ).start()

    left = {"S": ls, "D": ld}
    right = {"S": rs, "Q": rq, "D": rd, "W": rw}

    def left_step(stage, x, p):
        buf, h, a = left[x], HALF[p], OFFS[p]
        out = l_send.at[p]
        both = pl.ds(a, 2 * h)
        one, two = pl.ds(a, h), pl.ds(a + h, h)
        ones = (pl.ds(a, h // 2), pl.ds(a + h // 2, h // 2))
        twos = (pl.ds(a + h, h // 2), pl.ds(a + h + h // 2, h // 2))
        backs = (down, up)
        far_y, far_z = lax.rem(y + 2, 4), lax.rem(z + 2, 4)
        if stage == "a":
            if x == "S":
                start_rows(a, 2 * h)
            for axis in "yz":
                for side in (0, 1):
                    send(buf.at[z, y, both], to[axis, side], out, l_recv.at[4 * p])
        elif stage == "b":
            drain(buf.at[0, :, both], l_recv.at[4 * p])
            for side in (0, 1):
                send(buf.at[z, backs[side]["y"], ones[side]], to["y", side], out, l_recv.at[4 * p + 1])
                send(buf.at[backs[side]["z"], y, twos[side]], to["z", side], out, l_recv.at[4 * p + 1])
        elif stage == "x":
            for back in backs:
                for side in (0, 1):
                    send(buf.at[z, back["y"], one], to["z", side], out, l_recv.at[4 * p + 2])
                    send(buf.at[back["z"], y, two], to["y", side], out, l_recv.at[4 * p + 2])
        elif stage == "c":
            drain(buf.at[0, 0, both], l_recv.at[4 * p + 1])
            for side in (0, 1):
                send(buf.at[z, far_y, one], to["z", side], out, l_recv.at[4 * p + 2])
                send(buf.at[far_z, y, two], to["y", side], out, l_recv.at[4 * p + 2])
        elif stage == "d":
            drain(buf.at[pl.ds(0, 3), :, one], l_recv.at[4 * p + 2])
            for side in (0, 1):
                send(buf.at[backs[side]["z"], :, ones[side]], to["z", side], out, l_recv.at[4 * p + 3])
                send(buf.at[:, backs[side]["y"], twos[side]], to["y", side], out, l_recv.at[4 * p + 3])
        else:
            drain(buf.at[0, :, both], l_recv.at[4 * p + 3])

    def right_step(stage, x, p):
        buf = right[x]
        a, n = PIECES[p]
        out, near, far = r_send.at[p], r_recv.at[p], r_recv.at[NS + p]
        core = r_recv.at[2 * NS + 2 * p + "SQDW".index(x) % 2]
        rows = pl.ds(a, n)
        if stage == "a":
            if x == "S":
                start_rows(a, n)
            send(buf.at[r, rows], to["x", 0], out, near)
            send(buf.at[r, rows], to["x", 1], out, near)
            send(buf.at[r, rows], to["core"], out, core)
        elif stage == "b":
            drain(buf.at[pl.ds(0, 2), rows], near)
            send(buf.at[r_down, pl.ds(a, n // 2)], to["x", 0], out, far)
            send(buf.at[r_up, pl.ds(a + n // 2, n // 2)], to["x", 1], out, far)
            send(buf.at[r_down, rows], to["core"], out, core)
            send(buf.at[r_up, rows], to["core"], out, core)
        elif stage == "c":
            drain(buf.at[0, rows], far)
            send(buf.at[r_far, rows], to["core"], out, core)
        else:
            drain(buf.at[pl.ds(0, 4), rows], core)

    def all_sent():
        for p in range(NP):
            drain(ls.at[pl.ds(0, 3), :, pl.ds(0, 5 * HALF[p])], l_send.at[p])
        for p, (_, n) in enumerate(PIECES):
            drain(ls.at[:, :, pl.ds(0, 7 * n // 4)], r_send.at[p])

    def whole(buf, panel, a, n):
        rows = pl.ds(a, n)
        acc[rows, :] = jnp.zeros((n, COLS), F32)

        def step(i, _):
            lhs = jnp.concatenate([buf[i, j, rows, :] for j in range(4)], axis=1)
            rhs = panel[pl.ds(2 * i, 2)].reshape(4 * COLS, COLS)
            acc[rows, :] += jnp.dot(lhs, rhs, preferred_element_type=F32)
            return 0

        lax.fori_loop(0, 4, step, 0)

    def part(buf, panel, a, n, q):
        rows = pl.ds(a, n)
        lo, size = PART[q]
        group = 1024 // size

        def piece(i, j):
            zz = i * (group // 2) + j // 2
            cols = []
            for half in (0, 1):
                s, e = max(lo, half * COLS), min(lo + size, (half + 1) * COLS)
                if s < e:
                    cols.append(buf[zz, 2 * (j % 2) + half, rows, s - half * COLS : e - half * COLS])
            return cols

        def step(i, _):
            lhs = jnp.concatenate([v for j in range(group) for v in piece(i, j)], axis=1)
            rhs = panel[pl.ds(group * i, group), pl.ds(lo, size), :].reshape(1024, COLS)
            acc[rows, :] += jnp.dot(lhs, rhs, preferred_element_type=F32)
            return 0

        if q == 0:
            acc[rows, :] = jnp.zeros((n, COLS), F32)
        if NR == group:
            step(0, 0)
        else:
            lax.fori_loop(0, NR // group, step, 0)

    def fetch(i):
        if i < 3:
            rows = pl.ds(256 * i, 256)
            return pltpu.make_async_copy(ham.at[rows], fetched.at[0, rows], i_sem.at[i])
        src, dst = ((deriv, fetched.at[1]), (band_in, band), (frag_in, frag))[i - 3]
        return pltpu.make_async_copy(src, dst, i_sem.at[i])

    def split(buf, panel, early):
        h = HALF[LAST]
        one, two, both = pl.ds(OFFS[LAST], h), pl.ds(OFFS[LAST] + h, h), pl.ds(OFFS[LAST], 2 * h)
        zs, ys = (lax.rem(z + 2, 4), z, up["z"], down["z"]), (lax.rem(y + 2, 4), y, up["y"], down["y"])

        def add(rows, blocks):
            lhs = jnp.concatenate([buf[zz, yy, rows, :] for zz, yy in blocks], axis=1)
            half = [pl.ds(pl.multiple_of(lax.rem(yy, 2) * COLS, COLS), COLS) for _, yy in blocks]
            rhs = jnp.concatenate(
                [panel[2 * zz + lax.div(yy, 2), part_of, :] for (zz, yy), part_of in zip(blocks, half)], axis=0
            )
            acc[rows, :] += jnp.dot(lhs, rhs, preferred_element_type=F32)

        if early:
            acc[both, :] = jnp.zeros((2 * h, COLS), F32)

            def step(i, _):
                zz = lax.rem(z + i + lax.div(i, 2), 4)
                add(both, [(zz, yy) for yy in ys[1:]])
                return 0

            lax.fori_loop(0, 3, step, 0)
            add(one, [(zz, ys[0]) for zz in zs[1:]])
            add(two, [(zs[0], yy) for yy in ys[1:]])
        else:
            add(one, [(zs[0], yy) for yy in ys])
            add(two, [(zz, ys[0]) for zz in zs])

    first = int(ORDER[0][3])
    first = (OFFS if ORDER[0][0] == "L" else [a for a, _ in PIECES])[first] // 256
    order_of_rows = (first, *(i for i in range(3) if i != first))
    ready = {}

    def start_rows(a, n):
        for i in range(a // BLK, (a + n + BLK - 1) // BLK):
            if i in ready:
                continue
            if not ready:
                fetch(4).wait()
            if i // 2 not in ready.values():
                fetch(i // 2).wait()
            ready[i] = i // 2
            rows = pl.ds(i * BLK, BLK)
            for j in range(3):
                row, col, cols = r * 6 + i, c * 3 + j, pl.ds(j * BLK, BLK)
                inside = jnp.abs(row - col) <= jnp.maximum(band[row], band[col])
                block = jnp.full((BLK, BLK), jnp.where(inside, 1.0, 0.0), F32)
                mask[rows, cols] = block
                start = (fetched[0, rows, cols].astype(F32) * block).astype(BF16)
                rs[r, rows, cols] = start
                ls[z, y, rows, cols] = start

    def begin():
        for i in (4, *order_of_rows, 5, 3):
            fetch(i).start()
        terms[...] = jnp.zeros((8, COLS), F32)
        start_rows(256 * order_of_rows[0], 256)
        pl.semaphore_wait(barrier, len(to))

    def prepare():
        fetch(5).wait()
        for f in (0, 1):
            for j in range(3 * NC):
                weight = jnp.where(frag[j] == 2 * c + f, 1.0, 0.0)
                weights[f, j // 3, :, pl.ds(j % 3 * BLK, BLK)] = jnp.full((1, BLK), weight, F32)

    def square_rows(p):
        a, n = OFFS[p], 2 * HALF[p]
        if p == LAST:
            split(ls, rs, False)
        else:
            whole(ls, rs, a, n)
        rq[r, pl.ds(a, n), :] = (acc[pl.ds(a, n), :] * mask[pl.ds(a, n), :]).astype(BF16)

    def density_rows(p):
        a, n = OFFS[p], 2 * HALF[p]
        rows = pl.ds(a, n)
        sign = 1.5 * rs[r, rows, :].astype(F32) - 0.5 * acc[rows, :]
        sign = (mask[rows, :] * sign).astype(BF16)
        n_out[rows, :] = sign
        line = r * ROWS + a + lax.broadcasted_iota(jnp.int32, (n, COLS), 0)
        column = c * COLS + lax.broadcasted_iota(jnp.int32, (n, COLS), 1)
        identity = jnp.where(line == column, 1.0, 0.0)
        density = (0.5 * (identity - sign.astype(F32))).astype(BF16)
        rd[r, rows, :] = density
        ld[z, y, rows, :] = density

    def weighted_rows(u):
        rows = pl.ds(256 * u, 256)
        rw[r, rows, :] = (acc[rows, :] * mask[rows, :]).astype(BF16)

    def energy_rows(p):
        a, n = OFFS[p], 2 * HALF[p]
        rows = pl.ds(a, n)
        if p == FIRST:
            fetch(3).wait()
        energy = (acc[rows, :] * mask[rows, :]).astype(BF16)
        e_out[rows, :] = energy
        product = energy.astype(F32) * fetched[1, rows, :].astype(F32)
        terms[...] += jnp.sum(product.reshape(n // 8, 8, COLS), axis=0)

    def finish():
        mine[...] = jnp.sum(terms[...], axis=0, keepdims=True)
        by_row[r] = mine[...]
        for k in (4, 2, 6, 0):
            for other in (True, False):
                if k == 0 and not other:
                    continue
                peer = lax.rem(r + k, NR)
                peer = peer + 1 - 2 * lax.rem(r, 2) if other else peer
                pltpu.make_async_remote_copy(
                    src_ref=mine, dst_ref=by_row.at[r], send_sem=t_send.at[0], recv_sem=t_recv.at[0],
                    device_id=(peer, c), device_id_type=MESH,
                ).start()
        drain(by_row.at[pl.ds(0, NR - 1)], t_recv.at[0])
        by_col[c] = jnp.sum(by_row[...], axis=0)
        steps = sorted(range(1, NC), key=lambda k: -min(k // 4, 4 - k // 4) - min(k % 4, 4 - k % 4))
        for k in steps:
            peer = lax.rem(z + k // 4, 4) * 4 + lax.rem(y + k % 4, 4)
            send(by_col.at[c], (r, peer), t_send.at[1], t_recv.at[1])
        all_sent()
        drain(by_row.at[pl.ds(0, NR - 1)], t_send.at[0])
        drain(by_col.at[pl.ds(0, NC - 1)], t_recv.at[1])
        for f in (0, 1):
            picked = jnp.sum(weights[f] * by_col[...], axis=0)
            pulay[pl.ds(f, 1), :] = picked[:, :BLK] + picked[:, BLK : 2 * BLK] + picked[:, 2 * BLK :]
        drain(by_col.at[pl.ds(0, NC - 1)], t_send.at[1])

    begin()
    for name in ORDER:
        digits = [int(d) for d in name if d.isdigit()]
        if name[0] == "L":
            left_step(name[1], name[2], digits[0])
        elif name[0] == "R":
            right_step(name[1], name[2], digits[0])
        elif name[:3] in ("P1e", "P4e"):
            split(*((ls, rs) if name[1] == "1" else (ld, rw)), True)
        elif name[:2] == "P1":
            square_rows(digits[1])
        elif name[:2] in ("P2", "P3"):
            part(ls, rq if name[1] == "2" else rd, 256 * digits[1], 256, digits[2])
        elif name[:2] == "P4":
            p = digits[1]
            if len(digits) == 3:
                part(ld, rw, OFFS[p], 2 * HALF[p], digits[2])
            elif p == LAST:
                split(ld, rw, False)
            else:
                whole(ld, rw, OFFS[p], 2 * HALF[p])
        elif name[0] == "N":
            density_rows(digits[0])
        elif name[0] == "W":
            weighted_rows(digits[0])
        elif name[0] == "E":
            energy_rows(digits[0])
        else:
            prepare()
    finish()


def write_out(n_in, e_in, p_in, n_out, e_out, p_out, sems):
    copies = [
        pltpu.make_async_copy(src, dst, sems.at[i])
        for i, (src, dst) in enumerate(((n_in, n_out), (e_in, e_out), (p_in, p_out)))
    ]
    for copy in copies:
        copy.start()
    for copy in copies:
        copy.wait()


def step(ham, deriv, band, frag_of):
    vmem = pl.BlockSpec(memory_space=pltpu.VMEM)
    hbm = pl.BlockSpec(memory_space=pl.ANY)
    dma = pltpu.SemaphoreType.DMA
    panel = pltpu.VMEM((NR, ROWS, COLS), BF16)
    slab = pltpu.VMEM((4, 4, ROWS, COLS), BF16)
    shapes = (((ROWS, COLS), BF16), ((ROWS, COLS), BF16), ((2, BLK), F32))
    held = pl.pallas_call(
        kernel,
        out_shape=tuple(pltpu.VMEM(*shape) for shape in shapes),
        in_specs=[hbm, hbm, hbm, hbm],
        out_specs=(vmem, vmem, vmem),
        scratch_shapes=[
            slab, slab, panel, panel, panel, panel,
            pltpu.VMEM((ROWS, COLS), F32),
            pltpu.VMEM((ROWS, COLS), F32),
            pltpu.VMEM((8, COLS), F32),
            pltpu.VMEM((1, COLS), F32),
            pltpu.VMEM((NR, 1, COLS), F32),
            pltpu.VMEM((NC, 1, COLS), F32),
            pltpu.VMEM((2, NC, 1, COLS), F32),
            pltpu.VMEM((2, ROWS, COLS), BF16),
            pltpu.SMEM((6 * NR,), jnp.int32),
            pltpu.SMEM((6 * NR,), jnp.int32),
            dma((NP,)), dma((4 * NP,)), dma((NS,)), dma((4 * NS,)), dma((2,)), dma((2,)), dma((6,)),
        ],
        compiler_params=pltpu.CompilerParams(collective_id=0, has_side_effects=True, vmem_limit_bytes=56 << 20),
        name="sign_step",
    )(band, frag_of, ham, deriv)
    return pl.pallas_call(
        write_out,
        out_shape=tuple(jax.ShapeDtypeStruct(*shape) for shape in shapes),
        in_specs=[vmem, vmem, vmem],
        out_specs=(hbm, hbm, hbm),
        scratch_shapes=[dma((3,))],
        name="write_out",
    )(*(pltpu.with_memory_space_constraint(x, pltpu.VMEM) for x in held))


def solution(mesh):
    return jax.shard_map(
        step,
        mesh=mesh,
        in_specs=(P("row", "col"), P("row", "col"), P(), P()),
        out_specs=(P("row", "col"), P("row", "col"), P("col", None)),
        check_vma=False,
    )
```
